1024 devices in a mesh: elem: 32 (over y_lo, x, core), band: 32 (over z, y_hi).
Axes of the slice: x: 4, y: 8 (y_hi: 2, y_lo: 4; y = y_hi * 4 + y_lo), z: 16, core: 2. Of those that a mesh axis runs over, the one named last changes fastest.
Arguments:
- orbitals: float32 [128, 160, 1024], P('elem', 'band'), may hold values from -6 to 6
- rotation: float32 [1024, 1024], P('band'), may hold values from -0.375 to 0.375
- counts: int32 [128], P('elem'), may hold values from 96 to 160, as said below
- hamiltonian: float32 [128, 7, 160, 160], P('elem'), may hold values from -0.1875 to 0.1875
- filter_center: float32 [1], replicated, may hold values from -0.5 to 0.5
- filter_width: float32 [1], replicated, may hold values from 1.5 to 2.5
Outputs:
- filtered: float32 [128, 160, 1024], P('elem', None, 'band')
The draws below stay inside these ranges and needn't reach their ends.
Inputs may be any that keep to these rules, and one draw needn't show every extreme that they name: `counts`: some element has exactly 96 and some exactly 160 basis functions.
All inputs are finite; a program needn't handle non-finite values.
Results may differ from the reference program's by a relative error of at most 0.0001.
Values sent between devices are 32-bit elements; how exact they have to be, the bound alone decides.
No kernel may reach another device: no remote copies, remote signals or barrier semaphores. Data moves between devices by JAX's collectives and lax.ppermute only.
A program may use at most 32 MiB of HBM per device.

```python
import jax
import jax.numpy as jnp
from jax import lax

NB = 160
NBAND = 1024
GX = 4
GY = 8
CMIN = 96
GZ = 4
E = 128


def draw_counts(key, part):
    first, second, third = jax.random.split(jax.random.fold_in(key, 11), 3)
    values = jax.random.randint(first, (E,), CMIN, NB + 1, dtype=jnp.int32)
    high_spot = jax.random.randint(second, (), 0, E, dtype=jnp.int32)
    low_spot = (high_spot + 1 + jax.random.randint(third, (), 0, E - 1, dtype=jnp.int32)) % E
    values = values.at[high_spot].set(NB)
    values = values.at[low_spot].set(CMIN)
    return values


def raised(entries, stream_key, source, target, shards_of, factor):
    owner, partner = [(jnp.arange(entries.shape[axis_at]) // (entries.shape[axis_at] // shards_of)).reshape([-1 if axis == axis_at else 1 for axis in range(entries.ndim)]) for axis_at in (source, target)]
    chosen = jax.random.permutation(stream_key, shards_of)[partner]
    strong = (owner == chosen) | (owner == (partner + shards_of // 2) % shards_of)
    return jnp.where(strong, factor * entries, entries)


def levels(stream_key, extent, cuts, smallest, largest):
    gain, own = 1.0, jax.random.fold_in(stream_key, 6)
    for dim, parts in cuts:
        steps = jnp.exp(jax.random.uniform(jax.random.fold_in(own, dim), (parts,), jnp.float32, smallest / len(cuts), largest / len(cuts)))
        gain = gain * jnp.repeat(steps, extent[dim] // parts).reshape([-1 if axis == dim else 1 for axis in range(len(extent))])
    return gain


def bell_draw(stream_key, dims, scale, limit, pieces=(), kind=jnp.bfloat16):
    drawn = scale * jax.random.normal(stream_key, dims, jnp.float32)
    if pieces:
        drawn = drawn * levels(stream_key, dims, pieces, -0.22, 0.18)
    return jnp.clip(drawn, -limit, limit).astype(kind)


def noise_with(key, extent, spread, reach, pieces, heavy, kind=jnp.bfloat16):
    values = spread * jax.random.normal(key, extent, jnp.float32)
    if pieces:
        values = values * levels(key, extent, pieces, -0.22, 0.18)
    return jnp.clip(raised(values, jax.random.fold_in(key, 3), *heavy), -reach, reach).astype(kind)


def setup_inputs(seed: int = 0) -> dict:
    key_list = jax.random.split(jax.random.key(seed), 7)
    return {
        "orbitals": bell_draw(key_list[0], (E, NB, NBAND), 1.0, 6.0, ((0, 32), (1, 32)), jnp.float32),
        "rotation": noise_with(key_list[1], (NBAND, NBAND), NBAND ** -0.5, 0.375, ((0, 32),), (0, 1, 32, 2.75), jnp.float32),
        "counts": draw_counts(jax.random.fold_in(key_list[6], 71), 0),
        "hamiltonian": bell_draw(key_list[3], (E, 7, NB, NB), (7 * NB) ** -0.5, 0.1875, ((0, 32),), jnp.float32),
        "filter_center": jnp.clip(jax.random.uniform(key_list[4], (1,), jnp.float32, -0.5, 0.5), -0.5, 0.5),
        "filter_width": jnp.clip(jax.random.uniform(key_list[5], (1,), jnp.float32, 1.5, 2.5), 1.5, 2.5),
    }


def neighbour_fields(field):
    grid = field.reshape(GZ, GY, GX, NB, NBAND)
    zeros = jnp.zeros((1, GY, GX, NB, NBAND), jnp.float32)
    below = jnp.concatenate([zeros, grid[:-1]], axis=0)
    above = jnp.concatenate([grid[1:], zeros], axis=0)
    fields = [grid, jnp.roll(grid, 1, axis=2), jnp.roll(grid, -1, axis=2), jnp.roll(grid, 1, axis=1), jnp.roll(grid, -1, axis=1), below, above]
    return [f.reshape(E, NB, NBAND) for f in fields]


def apply_operator(field, hamiltonian, live):
    total = jnp.zeros((E, NB, NBAND), jnp.float32)
    for slot, other in enumerate(neighbour_fields(field)):
        total = total + jnp.einsum("erc,ecb->erb", hamiltonian[:, slot], other, precision=lax.Precision.HIGHEST)
    return jnp.where(live[:, :, None], total, jnp.float32(0.0))


def reference(orbitals, rotation, counts, hamiltonian, filter_center, filter_width):
    live = jnp.arange(NB, dtype=jnp.int32)[None, :] < counts[:, None]
    masked = jnp.where(live[:, :, None], orbitals, jnp.float32(0.0))
    start = jnp.einsum("eik,kb->eib", masked, rotation, precision=lax.Precision.HIGHEST)
    center = filter_center[0]
    width = filter_width[0]
    middle = (apply_operator(start, hamiltonian, live) - center * start) / width
    filtered = 2.0 * (apply_operator(middle, hamiltonian, live) - center * middle) / width - start
    return filtered
```

```python
import jax
import jax.numpy as jnp
from jax import lax
from jax.experimental import pallas as pl
from jax.experimental.pallas import tpu as pltpu
from jax.sharding import Mesh
from jax.sharding import PartitionSpec as P

LAYERS, COLUMNS, CORES = 4, 4, 2
FAR, NEAR = 4, 8
ELEMS, ROWS, WIDE = 4, 160, 128
BANDS = 32
PIECE = 5
ELEM = ("layer", "column", "core")
RING = ("column", "core")
NEARS = ("z_lo", "y_hi")
BAND = ("z_hi",) + NEARS
F32, BF16 = jnp.float32, jnp.bfloat16


def call(kernel, out, flops, moved, spaces):
    return pl.pallas_call(
        kernel,
        out_shape=jax.ShapeDtypeStruct(out, F32),
        in_specs=[pl.BlockSpec(memory_space=s) for s in spaces],
        out_specs=pl.BlockSpec(memory_space=pltpu.VMEM),
        compiler_params=pltpu.CompilerParams(vmem_limit_bytes=32 << 20),
        cost_estimate=pl.CostEstimate(flops=flops, bytes_accessed=moved, transcendentals=0),
    )


def split(v):
    high = v.astype(BF16)
    return high, (v - high.astype(F32)).astype(BF16)


def dot3(a, b):
    def dot(x, y):
        return jnp.dot(x, y, preferred_element_type=F32)

    return dot(a[0], b[0]) + (dot(a[0], b[1]) + dot(a[1], b[0]))


def lane_owner(shape):
    return lax.broadcasted_iota(jnp.int32, shape, len(shape) - 1) // BANDS


def by_owner(parts):
    owner = lane_owner(parts[0].shape)
    picked = parts[0]
    for e in range(1, ELEMS):
        picked = jnp.where(owner == e, parts[e], picked)
    return picked


def turned(v, by):
    by = by % ELEMS
    return pltpu.roll(v, by * BANDS, 1) if by else v


def alive(counts_ref):
    owner = lane_owner((ROWS, WIDE))
    row = lax.broadcasted_iota(jnp.int32, (ROWS, WIDE), 0)
    limit = jnp.full((ROWS, WIDE), counts_ref[0], jnp.int32)
    for e in range(1, ELEMS):
        limit = jnp.where(owner == e, counts_ref[e], limit)
    return row < limit


def cut_columns(orbitals_ref, out_ref):
    for i in range(PIECE):
        for near in range(NEAR):
            half, place = divmod(near, ELEMS)
            parts = [
                turned(orbitals_ref[i, :, pl.ds(256 * far + 128 * half, 128)], far - place)
                for far in range(FAR)
            ]
            out_ref[near, pl.ds(ELEMS * i, ELEMS), :] = by_owner(parts)


def pack(rows_ref, rotation_ref, out_ref):
    for e in range(ELEMS):
        for near in range(NEAR):
            for i in range(PIECE):
                out_ref[0, pl.ds(40 * e + PIECE * near + i, 1), :] = rows_ref[near, pl.ds(ELEMS * i + e, 1), :]
    rows = out_ref[0, :ROWS, :]
    for far in range(FAR):
        if far:
            out_ref[far, :ROWS, :] = rows
        out_ref[far, ROWS : ROWS + 32, :] = rotation_ref[:, pl.ds(256 * far, 128)]
        out_ref[far, ROWS + 32 :, :] = rotation_ref[:, pl.ds(256 * far + 128, 128)]


def rotate(packed_ref, out_ref):
    left = jnp.concatenate([packed_ref[far, ROWS : ROWS + 32, :] for far in range(FAR)], axis=0)
    right = jnp.concatenate([packed_ref[far, ROWS + 32 :, :] for far in range(FAR)], axis=0)
    halves = [split(left), split(right)]
    products = []
    for e in range(ELEMS):
        rows = jnp.concatenate([packed_ref[far, 40 * e : 40 * e + 40, :] for far in range(FAR)], axis=0)
        rows = split(rows)
        products.append([dot3(rows, half) for half in halves])
    for near in range(NEAR):
        half, place = divmod(near, ELEMS)
        out_ref[near] = by_owner([turned(products[e][half], e - place) for e in range(ELEMS)])


def add_up(parts_ref, counts_ref, out_ref):
    total = parts_ref[0]
    for near in range(1, NEAR):
        total = total + parts_ref[near]
    out_ref[...] = jnp.where(alive(counts_ref), total, 0.0)


def blocks_times(hamiltonian_ref, slots, fields):
    fields = [split(f) for f in fields]
    totals = []
    for e in range(ELEMS):
        total = None
        for slot, field in zip(slots, fields):
            term = dot3(split(hamiltonian_ref[e, slot]), field)
            total = term if total is None else total + term
        totals.append(total)
    return by_owner(totals)


def own_slots(field_ref, hamiltonian_ref, out_ref):
    field = field_ref[...]
    out_ref[...] = blocks_times(hamiltonian_ref, (0, 1, 2), (field, turned(field, 1), turned(field, -1)))


def first_step(own_ref, a_ref, b_ref, c_ref, d_ref, hamiltonian_ref, start_ref, counts_ref, center_ref, width_ref, out_ref):
    total = own_ref[...] + blocks_times(
        hamiltonian_ref, (3, 4, 5, 6), (a_ref[...], b_ref[...], c_ref[...], d_ref[...])
    )
    total = jnp.where(alive(counts_ref), total, 0.0)
    out_ref[...] = (total - center_ref[0] * start_ref[...]) / width_ref[0]


def second_step(own_ref, a_ref, b_ref, c_ref, d_ref, hamiltonian_ref, middle_ref, start_ref, counts_ref, center_ref, width_ref, out_ref):
    total = own_ref[...] + blocks_times(
        hamiltonian_ref, (3, 4, 5, 6), (a_ref[...], b_ref[...], c_ref[...], d_ref[...])
    )
    total = jnp.where(alive(counts_ref), total, 0.0)
    filtered = 2.0 * (total - center_ref[0] * middle_ref[...]) / width_ref[0] - start_ref[...]
    out_ref[...] = jnp.transpose(filtered)


def neighbours(field):
    ring = COLUMNS * CORES
    return (
        lax.ppermute(field, RING, [(i, (i + 1) % ring) for i in range(ring)]),
        lax.ppermute(field, RING, [(i, (i - 1) % ring) for i in range(ring)]),
        lax.ppermute(field, "layer", [(i, i + 1) for i in range(LAYERS - 1)]),
        lax.ppermute(field, "layer", [(i + 1, i) for i in range(LAYERS - 1)]),
    )


V, S = pltpu.VMEM, pltpu.SMEM
FIELD = ROWS * WIDE * 4
BLOCKS = ELEMS * 7 * ROWS * 256 * 4


def shards(orbitals, rotation, counts, hamiltonian, center, width):
    pieces = jnp.transpose(orbitals, (1, 0, 2))
    cut = call(cut_columns, (NEAR, ELEMS * PIECE, WIDE), 0, 2 * FIELD, (V,))(pieces)
    cut = lax.all_to_all(cut, NEARS, split_axis=0, concat_axis=0, tiled=True)
    packed = call(pack, (FAR, ROWS + 64, WIDE), 0, 6 * FIELD, (V, V))(cut, rotation)
    packed = lax.all_to_all(packed, "z_hi", split_axis=0, concat_axis=0, tiled=True)
    parts = call(rotate, (NEAR, ROWS, WIDE), 6 * 640 * 128 * 256, 13 * FIELD, (V,))(packed)
    parts = lax.all_to_all(parts, NEARS, split_axis=0, concat_axis=0, tiled=True)
    start = call(add_up, (ROWS, WIDE), 0, 9 * FIELD, (V, S))(parts, counts)

    own = call(own_slots, (ROWS, WIDE), 6 * 12 * ROWS * ROWS * WIDE, BLOCKS, (V, V))
    first = call(first_step, (ROWS, WIDE), 6 * 16 * ROWS * ROWS * WIDE, BLOCKS, (V,) * 7 + (S,) * 3)
    second = call(second_step, (WIDE, ROWS), 6 * 16 * ROWS * ROWS * WIDE, BLOCKS, (V,) * 8 + (S,) * 3)
    around = neighbours(start)
    middle = first(own(start, hamiltonian), *around, hamiltonian, start, counts, center, width)
    around = neighbours(middle)
    filtered = second(own(middle, hamiltonian), *around, hamiltonian, middle, start, counts, center, width)
    return jnp.transpose(filtered.reshape(ELEMS, BANDS, ROWS), (0, 2, 1))


def solution(mesh):
    inner = Mesh(
        mesh.devices.reshape(LAYERS, COLUMNS, CORES, FAR, NEAR // 2, 2), ELEM + BAND
    )
    return jax.shard_map(
        shards,
        mesh=inner,
        in_specs=(P(ELEM, BAND, None), P(BAND, None), P(ELEM), P(ELEM, None, None, None), P(), P()),
        out_specs=P(ELEM, None, BAND),
        check_vma=False,
    )
```

```python
import jax
import jax.numpy as jnp
from jax import lax
from jax.experimental import pallas as pl
from jax.experimental.pallas import tpu as pltpu
from jax.sharding import Mesh
from jax.sharding import PartitionSpec as P

LAYERS, COLUMNS, CORES = 4, 4, 2
FAR, NEAR = 4, 8
ELEMS, ROWS, WIDE = 4, 160, 128
BANDS = 32
PIECE = 5
ELEM = ("layer", "column", "core")
RING = ("column", "core")
NEARS = ("z_lo", "y_hi")
BAND = ("z_hi",) + NEARS
F32, BF16 = jnp.float32, jnp.bfloat16


def call(kernel, out, flops, moved, spaces):
    several = isinstance(out[0], tuple)
    shapes = tuple(jax.ShapeDtypeStruct(o, F32) for o in (out if several else (out,)))
    specs = tuple(pl.BlockSpec(memory_space=pltpu.VMEM) for _ in shapes)
    return pl.pallas_call(
        kernel,
        out_shape=shapes if several else shapes[0],
        in_specs=[pl.BlockSpec(memory_space=s) for s in spaces],
        out_specs=specs if several else specs[0],
        compiler_params=pltpu.CompilerParams(vmem_limit_bytes=32 << 20),
        cost_estimate=pl.CostEstimate(flops=flops, bytes_accessed=moved, transcendentals=0),
    )


def split(v):
    high = v.astype(BF16)
    return high, (v - high.astype(F32)).astype(BF16)


def dot3(a, b):
    def dot(x, y):
        return jnp.dot(x, y, preferred_element_type=F32)

    return dot(a[0], b[0]) + (dot(a[0], b[1]) + dot(a[1], b[0]))


def lane_owner(shape):
    return lax.broadcasted_iota(jnp.int32, shape, len(shape) - 1) // BANDS


def by_owner(parts):
    owner = lane_owner(parts[0].shape)
    picked = parts[0]
    for e in range(1, ELEMS):
        picked = jnp.where(owner == e, parts[e], picked)
    return picked


def turned(v, by):
    by = by % ELEMS
    return pltpu.roll(v, by * BANDS, 1) if by else v


def alive(counts_ref):
    owner = lane_owner((ROWS, WIDE))
    row = lax.broadcasted_iota(jnp.int32, (ROWS, WIDE), 0)
    limit = jnp.full((ROWS, WIDE), counts_ref[0], jnp.int32)
    for e in range(1, ELEMS):
        limit = jnp.where(owner == e, counts_ref[e], limit)
    return row < limit


def cut_columns(orbitals_ref, rotation_ref, counts_ref, out_ref, slices_ref, live_ref):
    live_ref[...] = jnp.where(alive(counts_ref), 1.0, 0.0)
    for far in range(FAR):
        for half in range(2):
            slices_ref[far, pl.ds(32 * half, 32), :] = rotation_ref[:, pl.ds(256 * far + 128 * half, 128)]
    for i in range(PIECE):
        for near in range(NEAR):
            half, place = divmod(near, ELEMS)
            parts = [
                turned(orbitals_ref[i, :, pl.ds(256 * far + 128 * half, 128)], far - place)
                for far in range(FAR)
            ]
            out_ref[near, pl.ds(ELEMS * i, ELEMS), :] = by_owner(parts)


def pack(rows_ref, slices_ref, out_ref):
    for e in range(ELEMS):
        for near in range(NEAR):
            for i in range(PIECE):
                out_ref[0, pl.ds(40 * e + PIECE * near + i, 1), :] = rows_ref[near, pl.ds(ELEMS * i + e, 1), :]
    rows = out_ref[0, :ROWS, :]
    for far in range(FAR):
        if far:
            out_ref[far, :ROWS, :] = rows
        out_ref[far, ROWS:, :] = slices_ref[far]


def rotate(packed_ref, out_ref):
    left = jnp.concatenate([packed_ref[far, ROWS : ROWS + 32, :] for far in range(FAR)], axis=0)
    right = jnp.concatenate([packed_ref[far, ROWS + 32 :, :] for far in range(FAR)], axis=0)
    halves = [split(left), split(right)]
    products = []
    for e in range(ELEMS):
        rows = jnp.concatenate([packed_ref[far, 40 * e : 40 * e + 40, :] for far in range(FAR)], axis=0)
        rows = split(rows)
        products.append([dot3(rows, half) for half in halves])
    for near in range(NEAR):
        half, place = divmod(near, ELEMS)
        out_ref[near] = by_owner([turned(products[e][half], e - place) for e in range(ELEMS)])


def add_up(parts_ref, live_ref, out_ref):
    total = parts_ref[0]
    for near in range(1, NEAR):
        total = total + parts_ref[near]
    out_ref[...] = jnp.where(live_ref[...] > 0.5, total, 0.0)


def blocks_times(hamiltonian_ref, slots, fields):
    def dot(x, y):
        return jnp.dot(x, y, preferred_element_type=F32)

    fields = [split(f) for f in fields]
    pairs = [jnp.concatenate(f, axis=1) for f in fields]
    totals = []
    for e in range(ELEMS):
        wide = narrow = None
        for slot, field, pair in zip(slots, fields, pairs):
            high, low = split(hamiltonian_ref[e, slot])
            first, second = dot(high, pair), dot(low, field[0])
            wide = first if wide is None else wide + first
            narrow = second if narrow is None else narrow + second
        totals.append(wide[:, :WIDE] + (wide[:, WIDE:] + narrow))
    return by_owner(totals)


def own_and_ring(field_ref, a_ref, b_ref, hamiltonian_ref, out_ref):
    field = field_ref[...]
    out_ref[...] = blocks_times(
        hamiltonian_ref, range(5), (field, turned(field, 1), turned(field, -1), a_ref[...], b_ref[...])
    )


def applied(own_ref, c_ref, d_ref, hamiltonian_ref, live_ref):
    total = own_ref[...] + blocks_times(hamiltonian_ref, (5, 6), (c_ref[...], d_ref[...]))
    return jnp.where(live_ref[...] > 0.5, total, 0.0)


def first_step(own_ref, c_ref, d_ref, hamiltonian_ref, start_ref, live_ref, center_ref, width_ref, out_ref):
    total = applied(own_ref, c_ref, d_ref, hamiltonian_ref, live_ref)
    out_ref[...] = (total - center_ref[0] * start_ref[...]) / width_ref[0]


def second_step(own_ref, c_ref, d_ref, hamiltonian_ref, middle_ref, start_ref, live_ref, center_ref, width_ref, out_ref):
    total = applied(own_ref, c_ref, d_ref, hamiltonian_ref, live_ref)
    filtered = 2.0 * (total - center_ref[0] * middle_ref[...]) / width_ref[0] - start_ref[...]
    out_ref[...] = jnp.transpose(filtered)


def neighbours(field):
    ring = COLUMNS * CORES
    return (
        lax.ppermute(field, RING, [(i, (i + 1) % ring) for i in range(ring)]),
        lax.ppermute(field, RING, [(i, (i - 1) % ring) for i in range(ring)]),
        lax.ppermute(field, "layer", [(i, i + 1) for i in range(LAYERS - 1)]),
        lax.ppermute(field, "layer", [(i + 1, i) for i in range(LAYERS - 1)]),
    )


V, S = pltpu.VMEM, pltpu.SMEM
FIELD = ROWS * WIDE * 4
BLOCKS = ELEMS * 7 * ROWS * 256 * 4


def shards(orbitals, rotation, counts, hamiltonian, center, width):
    pieces = jnp.transpose(orbitals, (1, 0, 2))
    shapes = ((NEAR, ELEMS * PIECE, WIDE), (FAR, 64, WIDE), (ROWS, WIDE))
    cut, slices, live = call(cut_columns, shapes, 0, 6 * FIELD, (V, V, S))(pieces, rotation, counts)
    cut = lax.all_to_all(cut, NEARS, split_axis=0, concat_axis=0, tiled=True)
    packed = call(pack, (FAR, ROWS + 64, WIDE), 0, 6 * FIELD, (V, V))(cut, slices)
    packed = lax.all_to_all(packed, "z_hi", split_axis=0, concat_axis=0, tiled=True)
    parts = call(rotate, (NEAR, ROWS, WIDE), 6 * 640 * 128 * 256, 13 * FIELD, (V,))(packed)
    parts = lax.all_to_all(parts, NEARS, split_axis=0, concat_axis=0, tiled=True)
    start = call(add_up, (ROWS, WIDE), 0, 9 * FIELD, (V, V))(parts, live)

    own = call(own_and_ring, (ROWS, WIDE), 6 * 20 * ROWS * ROWS * WIDE, BLOCKS, (V,) * 4)
    first = call(first_step, (ROWS, WIDE), 6 * 8 * ROWS * ROWS * WIDE, BLOCKS // 3, (V,) * 6 + (S,) * 2)
    second = call(second_step, (WIDE, ROWS), 6 * 8 * ROWS * ROWS * WIDE, BLOCKS // 3, (V,) * 7 + (S,) * 2)
    a, b, c, d = neighbours(start)
    own_part = own(start, a, b, hamiltonian)
    middle = first(own_part, c, d, hamiltonian, start, live, center, width)
    a, b, c, d = neighbours(middle)
    own_part = own(middle, a, b, hamiltonian)
    filtered = second(own_part, c, d, hamiltonian, middle, start, live, center, width)
    return jnp.transpose(filtered.reshape(ELEMS, BANDS, ROWS), (0, 2, 1))


def solution(mesh):
    inner = Mesh(
        mesh.devices.reshape(LAYERS, COLUMNS, CORES, FAR, NEAR // 2, 2), ELEM + BAND
    )
    return jax.shard_map(
        shards,
        mesh=inner,
        in_specs=(P(ELEM, BAND, None), P(BAND, None), P(ELEM), P(ELEM, None, None, None), P(), P()),
        out_specs=P(ELEM, None, BAND),
        check_vma=False,
    )
```

```python
import jax
import jax.numpy as jnp
from jax import lax
from jax.experimental import pallas as pl
from jax.experimental.pallas import tpu as pltpu
from jax.sharding import Mesh
from jax.sharding import PartitionSpec as P

LAYERS, COLUMNS, CORES = 4, 4, 2
FAR, NEAR = 4, 8
ELEMS, ROWS, WIDE = 4, 160, 128
BANDS = 32
PIECE = 5
ELEM = ("layer", "column", "core")
RING = ("column", "core")
NEARS = ("z_lo", "y_hi")
BAND = ("z_hi",) + NEARS
F32, BF16 = jnp.float32, jnp.bfloat16


def call(kernel, out, flops, moved, spaces, scratch=(), kind=F32):
    several = isinstance(out[0], tuple)
    shapes = tuple(jax.ShapeDtypeStruct(o, kind) for o in (out if several else (out,)))
    specs = tuple(pl.BlockSpec(memory_space=pltpu.VMEM) for _ in shapes)
    return pl.pallas_call(
        kernel,
        out_shape=shapes if several else shapes[0],
        in_specs=[pl.BlockSpec(memory_space=s) for s in spaces],
        out_specs=specs if several else specs[0],
        scratch_shapes=scratch,
        compiler_params=pltpu.CompilerParams(vmem_limit_bytes=32 << 20),
        cost_estimate=pl.CostEstimate(flops=flops, bytes_accessed=moved, transcendentals=0),
    )


def split(v):
    high = v.astype(BF16)
    return high, (v - high.astype(F32)).astype(BF16)


def dot3(a, b):
    def dot(x, y):
        return jnp.dot(x, y, preferred_element_type=F32)

    return dot(a[0], b[0]) + (dot(a[0], b[1]) + dot(a[1], b[0]))


def lane_owner(shape):
    return lax.broadcasted_iota(jnp.int32, shape, len(shape) - 1) // BANDS


def by_owner(parts):
    owner = lane_owner(parts[0].shape)
    picked = parts[0]
    for e in range(1, ELEMS):
        picked = jnp.where(owner == e, parts[e], picked)
    return picked


def turned(v, by):
    by = by % ELEMS
    return pltpu.roll(v, by * BANDS, 1) if by else v


def alive(counts_ref):
    owner = lane_owner((ROWS, WIDE))
    row = lax.broadcasted_iota(jnp.int32, (ROWS, WIDE), 0)
    limit = jnp.full((ROWS, WIDE), counts_ref[0], jnp.int32)
    for e in range(1, ELEMS):
        limit = jnp.where(owner == e, counts_ref[e], limit)
    return row < limit


def cut_columns(orbitals_ref, rotation_ref, counts_ref, out_ref, slices_ref, live_ref):
    live_ref[...] = jnp.where(alive(counts_ref), 1.0, 0.0)
    for far in range(FAR):
        for half in range(2):
            slices_ref[far, pl.ds(32 * half, 32), :] = rotation_ref[:, pl.ds(256 * far + 128 * half, 128)]
    for i in range(PIECE):
        for near in range(NEAR):
            half, place = divmod(near, ELEMS)
            parts = [
                turned(orbitals_ref[i, :, pl.ds(256 * far + 128 * half, 128)], far - place)
                for far in range(FAR)
            ]
            out_ref[near, pl.ds(ELEMS * i, ELEMS), :] = by_owner(parts)


def far_place(by):
    return lax.rem(lax.axis_index("z_hi") + by, FAR)


HALF = ROWS // 2
PASS = HALF + 32


def pack(rows_ref, slices_ref, up_ref, down_ref):
    for e in range(ELEMS):
        top, mine = divmod(e, 2)
        first, second = (down_ref, up_ref) if top else (up_ref, down_ref)
        for near in range(NEAR):
            for i in range(PIECE):
                at = 40 * mine + PIECE * near + i
                row = rows_ref[near, pl.ds(ELEMS * i + e, 1), :]
                first[pl.ds(at, 1), :] = row
                second[pl.ds(PASS + at, 1), :] = row
    opposite = far_place(2)
    up_ref[HALF:PASS, :] = slices_ref[opposite, :32, :]
    down_ref[HALF:PASS, :] = slices_ref[opposite, 32:, :]
    up_ref[PASS + HALF :, :] = slices_ref[far_place(1)]
    down_ref[PASS + HALF :, :] = slices_ref[far_place(3)]


def rotate(up_ref, down_ref, slices_ref, below_ref, above_ref, passed_up_ref, passed_down_ref, out_ref, left_ref, right_ref):
    own = slices_ref[far_place(0)]
    sides = [
        (0, own[:32], own[32:], up_ref[:HALF, :], down_ref[:HALF, :]),
        (3, below_ref[PASS + HALF : PASS + HALF + 32, :], below_ref[PASS + HALF + 32 :, :],
         below_ref[:HALF, :], below_ref[PASS : PASS + HALF, :]),
        (1, above_ref[PASS + HALF : PASS + HALF + 32, :], above_ref[PASS + HALF + 32 :, :],
         above_ref[PASS : PASS + HALF, :], above_ref[:HALF, :]),
        (2, passed_up_ref[HALF:, :], passed_down_ref[HALF:, :], passed_up_ref[:HALF, :], passed_down_ref[:HALF, :]),
    ]
    for by, left, right, _, _ in sides:
        at = pl.ds(pl.multiple_of(32 * far_place(by), 32), 32)
        left_ref[at, :] = left
        right_ref[at, :] = right
    halves = [split(left_ref[...]), split(right_ref[...])]
    for by, _, _, top, bottom in sides:
        rows = split(jnp.concatenate([top, bottom], axis=0))
        products = [dot3(rows, half) for half in halves]
        at = pl.ds(pl.multiple_of(40 * far_place(by), 8), 40)
        for near in range(NEAR):
            half, place = divmod(near, ELEMS)
            out_ref[near, at, :] = by_owner(
                [turned(products[half][40 * e : 40 * e + 40], e - place) for e in range(ELEMS)]
            )


def add_up(parts_ref, live_ref, out_ref):
    total = parts_ref[0]
    for near in range(1, NEAR):
        total = total + parts_ref[near]
    out_ref[...] = jnp.where(live_ref[...] > 0.5, total, 0.0)


def split_blocks(hamiltonian_ref, high_ref, low_ref):
    for e in range(ELEMS):
        for slot in range(7):
            high_ref[e, slot], low_ref[e, slot] = split(hamiltonian_ref[e, slot])


def blocks_times(high_ref, low_ref, slots, fields):
    def dot(x, y):
        return jnp.dot(x, y, preferred_element_type=F32)

    fields = [split(f) for f in fields]
    pairs = [jnp.concatenate(f, axis=1) for f in fields]
    totals = []
    for e in range(ELEMS):
        wide = narrow = None
        for slot, field, pair in zip(slots, fields, pairs):
            first, second = dot(high_ref[e, slot], pair), dot(low_ref[e, slot], field[0])
            wide = first if wide is None else wide + first
            narrow = second if narrow is None else narrow + second
        totals.append(wide[:, :WIDE] + (wide[:, WIDE:] + narrow))
    return by_owner(totals)


def own_and_ring(field_ref, a_ref, b_ref, high_ref, low_ref, out_ref):
    field = field_ref[...]
    out_ref[...] = blocks_times(
        high_ref, low_ref, range(5), (field, turned(field, 1), turned(field, -1), a_ref[...], b_ref[...])
    )


def applied(own_ref, c_ref, d_ref, high_ref, low_ref, live_ref):
    total = own_ref[...] + blocks_times(high_ref, low_ref, (5, 6), (c_ref[...], d_ref[...]))
    return jnp.where(live_ref[...] > 0.5, total, 0.0)


def first_step(own_ref, c_ref, d_ref, high_ref, low_ref, start_ref, live_ref, center_ref, width_ref, out_ref):
    total = applied(own_ref, c_ref, d_ref, high_ref, low_ref, live_ref)
    out_ref[...] = (total - center_ref[0] * start_ref[...]) / width_ref[0]


def second_step(own_ref, c_ref, d_ref, high_ref, low_ref, middle_ref, start_ref, live_ref, center_ref, width_ref, out_ref):
    total = applied(own_ref, c_ref, d_ref, high_ref, low_ref, live_ref)
    filtered = 2.0 * (total - center_ref[0] * middle_ref[...]) / width_ref[0] - start_ref[...]
    out_ref[...] = jnp.transpose(filtered)


def neighbours(field):
    ring = COLUMNS * CORES
    return (
        lax.ppermute(field, RING, [(i, (i + 1) % ring) for i in range(ring)]),
        lax.ppermute(field, RING, [(i, (i - 1) % ring) for i in range(ring)]),
        lax.ppermute(field, "layer", [(i, i + 1) for i in range(LAYERS - 1)]),
        lax.ppermute(field, "layer", [(i + 1, i) for i in range(LAYERS - 1)]),
    )


def far_step(v, by):
    return lax.ppermute(v, "z_hi", [(i, (i + by) % FAR) for i in range(FAR)])


V, S = pltpu.VMEM, pltpu.SMEM
FIELD = ROWS * WIDE * 4
BLOCKS = ELEMS * 7 * ROWS * 256 * 4


def shards(orbitals, rotation, counts, hamiltonian, center, width):
    pieces = jnp.transpose(orbitals, (1, 0, 2))
    shapes = ((NEAR, ELEMS * PIECE, WIDE), (FAR, 64, WIDE), (ROWS, WIDE))
    cut, slices, live = call(cut_columns, shapes, 0, 6 * FIELD, (V, V, S))(pieces, rotation, counts)
    cut = lax.all_to_all(cut, NEARS, split_axis=0, concat_axis=0, tiled=True)
    message = (2 * PASS + 32, WIDE)
    up, down = call(pack, (message, message), 0, 6 * FIELD, (V, V))(cut, slices)
    above, below = far_step(down, -1), far_step(up, 1)
    passed_up, passed_down = far_step(below[:PASS], 1), far_step(above[:PASS], -1)
    blocks = call(split_blocks, (hamiltonian.shape,) * 2, 0, 2 * BLOCKS, (V,), (), BF16)(hamiltonian)
    slices, *blocks = lax.optimization_barrier((slices, *blocks))
    scratch = [V((WIDE, WIDE), F32)] * 2
    parts = call(rotate, (NEAR, ROWS, WIDE), 6 * 640 * 128 * 256, 13 * FIELD, (V,) * 7, scratch)(
        up, down, slices, below, above, passed_up, passed_down
    )
    parts = lax.all_to_all(parts, NEARS, split_axis=0, concat_axis=0, tiled=True)
    start = call(add_up, (ROWS, WIDE), 0, 9 * FIELD, (V, V))(parts, live)

    own = call(own_and_ring, (ROWS, WIDE), 6 * 20 * ROWS * ROWS * WIDE, BLOCKS, (V,) * 5)
    first = call(first_step, (ROWS, WIDE), 6 * 8 * ROWS * ROWS * WIDE, BLOCKS // 3, (V,) * 7 + (S,) * 2)
    second = call(second_step, (WIDE, ROWS), 6 * 8 * ROWS * ROWS * WIDE, BLOCKS // 3, (V,) * 8 + (S,) * 2)
    a, b, c, d = neighbours(start)
    own_part = own(start, a, b, *blocks)
    middle = first(own_part, c, d, *blocks, start, live, center, width)
    a, b, c, d = neighbours(middle)
    own_part = own(middle, a, b, *blocks)
    filtered = second(own_part, c, d, *blocks, middle, start, live, center, width)
    return jnp.transpose(filtered.reshape(ELEMS, BANDS, ROWS), (0, 2, 1))


def solution(mesh):
    inner = Mesh(
        mesh.devices.reshape(LAYERS, COLUMNS, CORES, FAR, NEAR // 2, 2), ELEM + BAND
    )
    return jax.shard_map(
        shards,
        mesh=inner,
        in_specs=(P(ELEM, BAND, None), P(BAND, None), P(ELEM), P(ELEM, None, None, None), P(), P()),
        out_specs=P(ELEM, None, BAND),
        check_vma=False,
    )
```

```python
import jax
import jax.numpy as jnp
from jax import lax
from jax.experimental import pallas as pl
from jax.experimental.pallas import tpu as pltpu
from jax.sharding import Mesh
from jax.sharding import PartitionSpec as P

LAYERS, COLUMNS, CORES = 4, 4, 2
FAR, LOW, NEAR = 4, 4, 8
ELEMS, ROWS, WIDE = 4, 160, 128
BANDS = 32
PIECE = 5
ELEM = ("layer", "column", "core")
RING = ("column", "core")
NEARS = ("z_lo", "y_hi")
BAND = ("z_hi",) + NEARS
F32, BF16 = jnp.float32, jnp.bfloat16


def call(kernel, out, flops, moved, spaces, scratch=(), kind=F32):
    several = isinstance(out[0], tuple)
    shapes = tuple(jax.ShapeDtypeStruct(o, kind) for o in (out if several else (out,)))
    specs = tuple(pl.BlockSpec(memory_space=pltpu.VMEM) for _ in shapes)
    return pl.pallas_call(
        kernel,
        out_shape=shapes if several else shapes[0],
        in_specs=[pl.BlockSpec(memory_space=s) for s in spaces],
        out_specs=specs if several else specs[0],
        scratch_shapes=scratch,
        compiler_params=pltpu.CompilerParams(vmem_limit_bytes=32 << 20),
        cost_estimate=pl.CostEstimate(flops=flops, bytes_accessed=moved, transcendentals=0),
    )


def split(v):
    high = v.astype(BF16)
    return high, (v - high.astype(F32)).astype(BF16)


def dot3(a, b):
    def dot(x, y):
        return jnp.dot(x, y, preferred_element_type=F32)

    return dot(a[0], b[0]) + (dot(a[0], b[1]) + dot(a[1], b[0]))


def lane_owner(shape):
    return lax.broadcasted_iota(jnp.int32, shape, len(shape) - 1) // BANDS


def by_owner(parts):
    owner = lane_owner(parts[0].shape)
    picked = parts[0]
    for e in range(1, ELEMS):
        picked = jnp.where(owner == e, parts[e], picked)
    return picked


def turned(v, by):
    by = by % ELEMS
    return pltpu.roll(v, by * BANDS, 1) if by else v


def alive(counts_ref):
    owner = lane_owner((ROWS, WIDE))
    row = lax.broadcasted_iota(jnp.int32, (ROWS, WIDE), 0)
    limit = jnp.full((ROWS, WIDE), counts_ref[0], jnp.int32)
    for e in range(1, ELEMS):
        limit = jnp.where(owner == e, counts_ref[e], limit)
    return row < limit


def cut_columns(orbitals_ref, counts_ref, out_ref, live_ref):
    live_ref[...] = jnp.where(alive(counts_ref), 1.0, 0.0)
    first = lax.broadcasted_iota(jnp.int32, (ELEMS, WIDE), 1) < 64
    for i in range(PIECE):
        for low in range(LOW):
            half, odd = divmod(low, 2)
            for k in range(2):
                parts = [orbitals_ref[i, :, pl.ds(256 * far + 128 * half, 128)] for far in (2 * k, 2 * k + 1)]
                parts[1 - odd] = turned(parts[1 - odd], 2)
                out_ref[low, pl.ds(20 * k + ELEMS * i, ELEMS), :] = jnp.where(first, parts[0], parts[1])


def far_place(by):
    return lax.rem(lax.axis_index("z_hi") + by, FAR)


HALF = ROWS // 2
PASS = HALF + 64


def pack(rows_ref, mine_ref, other_ref, up_ref, down_ref, own_ref):
    for k in range(2):
        first, second = (down_ref, up_ref) if k else (up_ref, down_ref)
        for e in range(ELEMS):
            for low in range(LOW):
                for i in range(PIECE):
                    at = 20 * e + PIECE * low + i
                    row = rows_ref[low, pl.ds(20 * k + ELEMS * i + e, 1), :]
                    first[pl.ds(at, 1), :] = row
                    second[pl.ds(PASS + at, 1), :] = row
    here = lax.axis_index("y_hi")
    for place, ref in ((here, mine_ref), (1 - here, other_ref)):

        def put(to, start, far, half):
            lanes = pl.ds(pl.multiple_of(256 * far + 128 * half, 128), 128)
            to[pl.ds(pl.multiple_of(start + 32 * place, 16), 32), :] = ref[:, lanes]

        put(up_ref, HALF, far_place(2), 0)
        put(down_ref, HALF, far_place(2), 1)
        for half in range(2):
            put(up_ref, PASS + HALF + 64 * half, far_place(1), half)
            put(down_ref, PASS + HALF + 64 * half, far_place(3), half)
            put(own_ref, 64 * half, far_place(0), half)


def rotate(
    up_ref, down_ref, own_ref, below_ref, above_ref, passed_up_ref, passed_down_ref, out_ref, left_ref, right_ref, sum_ref
):
    tail = PASS + HALF
    sides = [
        (0, own_ref[:64, :], own_ref[64:, :], up_ref[:HALF, :], down_ref[:HALF, :]),
        (3, below_ref[tail : tail + 64, :], below_ref[tail + 64 :, :], below_ref[:HALF, :], below_ref[PASS:tail, :]),
        (1, above_ref[tail : tail + 64, :], above_ref[tail + 64 :, :], above_ref[PASS:tail, :], above_ref[:HALF, :]),
        (2, passed_up_ref[HALF:, :], passed_down_ref[HALF:, :], passed_up_ref[:HALF, :], passed_down_ref[:HALF, :]),
    ]
    for by, left, right, _, _ in sides:
        at = pl.ds(pl.multiple_of(64 * far_place(by), 64), 64)
        left_ref[at, :] = left
        right_ref[at, :] = right
    halves = [split(left_ref[...]), split(right_ref[...])]
    for by, _, _, top, bottom in sides:
        rows = split(jnp.concatenate([top, bottom], axis=1))
        for half in range(2):
            sum_ref[half] = dot3(rows, halves[half])
        for near in range(NEAR):
            half, place = divmod(near, ELEMS)
            out_ref[near, pl.ds(20 * by, 20), :] = by_owner(
                [turned(sum_ref[half, pl.ds(20 * e, 20), :], e - place) for e in range(ELEMS)]
            )


def add_up(parts_ref, live_ref, out_ref, sum_ref, rows_ref):
    for share in range(2):
        total = parts_ref[share]
        for low in range(1, LOW):
            total = total + parts_ref[2 * low + share]
        sum_ref[share] = total
    for by in range(FAR):
        for share in range(2):
            for low in range(LOW):
                rows_ref[pl.ds(10 * low + PIECE * share, PIECE), :] = sum_ref[share, pl.ds(20 * by + PIECE * low, PIECE), :]
        at = pl.ds(pl.multiple_of(40 * far_place(by), 8), 40)
        out_ref[at, :] = jnp.where(live_ref[at, :] > 0.5, rows_ref[...], 0.0)


def split_blocks(hamiltonian_ref, high_ref, low_ref):
    for e in range(ELEMS):
        for slot in range(7):
            high_ref[e, slot], low_ref[e, slot] = split(hamiltonian_ref[e, slot])


def blocks_times(high_ref, low_ref, slots, fields):
    def dot(x, y):
        return jnp.dot(x, y, preferred_element_type=F32)

    fields = [split(f) for f in fields]
    pairs = [jnp.concatenate(f, axis=1) for f in fields]
    totals = []
    for e in range(ELEMS):
        wide = narrow = None
        for slot, field, pair in zip(slots, fields, pairs):
            first, second = dot(high_ref[e, slot], pair), dot(low_ref[e, slot], field[0])
            wide = first if wide is None else wide + first
            narrow = second if narrow is None else narrow + second
        totals.append(wide[:, :WIDE] + (wide[:, WIDE:] + narrow))
    return by_owner(totals)


def own_and_ring(field_ref, a_ref, b_ref, high_ref, low_ref, out_ref):
    field = field_ref[...]
    out_ref[...] = blocks_times(
        high_ref, low_ref, range(5), (field, turned(field, 1), turned(field, -1), a_ref[...], b_ref[...])
    )


def applied(own_ref, c_ref, d_ref, high_ref, low_ref, live_ref):
    total = own_ref[...] + blocks_times(high_ref, low_ref, (5, 6), (c_ref[...], d_ref[...]))
    return jnp.where(live_ref[...] > 0.5, total, 0.0)


def first_step(own_ref, c_ref, d_ref, high_ref, low_ref, start_ref, live_ref, center_ref, width_ref, out_ref):
    total = applied(own_ref, c_ref, d_ref, high_ref, low_ref, live_ref)
    out_ref[...] = (total - center_ref[0] * start_ref[...]) / width_ref[0]


def second_step(own_ref, c_ref, d_ref, high_ref, low_ref, middle_ref, start_ref, live_ref, center_ref, width_ref, out_ref):
    total = applied(own_ref, c_ref, d_ref, high_ref, low_ref, live_ref)
    filtered = 2.0 * (total - center_ref[0] * middle_ref[...]) / width_ref[0] - start_ref[...]
    out_ref[...] = jnp.transpose(filtered)


def neighbours(field):
    ring = COLUMNS * CORES
    return (
        lax.ppermute(field, RING, [(i, (i + 1) % ring) for i in range(ring)]),
        lax.ppermute(field, RING, [(i, (i - 1) % ring) for i in range(ring)]),
        lax.ppermute(field, "layer", [(i, i + 1) for i in range(LAYERS - 1)]),
        lax.ppermute(field, "layer", [(i + 1, i) for i in range(LAYERS - 1)]),
    )


def far_step(v, by):
    return lax.ppermute(v, "z_hi", [(i, (i + by) % FAR) for i in range(FAR)])


V, S = pltpu.VMEM, pltpu.SMEM
FIELD = ROWS * WIDE * 4
BLOCKS = ELEMS * 7 * ROWS * 256 * 4


def shards(orbitals, rotation, counts, hamiltonian, center, width):
    pieces = jnp.transpose(orbitals, (1, 0, 2))
    other = lax.ppermute(rotation, "y_hi", [(0, 1), (1, 0)])
    cut, live = call(cut_columns, ((LOW, 2 * ELEMS * PIECE, WIDE), (ROWS, WIDE)), 0, 3 * FIELD, (V, S))(pieces, counts)
    cut = lax.all_to_all(cut, "z_lo", split_axis=0, concat_axis=0, tiled=True)
    message = (2 * PASS + 64, WIDE)
    up, down, slices = call(pack, (message, message, (WIDE, WIDE)), 0, 8 * FIELD, (V,) * 3)(cut, rotation, other)
    above, below = far_step(down, -1), far_step(up, 1)
    passed_up, passed_down = far_step(below[:PASS], 1), far_step(above[:PASS], -1)
    blocks = call(split_blocks, (hamiltonian.shape,) * 2, 0, 2 * BLOCKS, (V,), (), BF16)(hamiltonian)
    slices, *blocks = lax.optimization_barrier((slices, *blocks))
    scratch = [V((256, WIDE), F32)] * 2 + [V((2, HALF, WIDE), F32)]
    parts = call(rotate, (NEAR, HALF, WIDE), 6 * 320 * 256 * 256, 11 * FIELD, (V,) * 7, scratch)(
        up, down, slices, below, above, passed_up, passed_down
    )
    parts = lax.all_to_all(parts, NEARS, split_axis=0, concat_axis=0, tiled=True)
    scratch = [V((2, HALF, WIDE), F32), V((40, WIDE), F32)]
    start = call(add_up, (ROWS, WIDE), 0, 5 * FIELD, (V, V), scratch)(parts, live)

    own = call(own_and_ring, (ROWS, WIDE), 6 * 20 * ROWS * ROWS * WIDE, BLOCKS, (V,) * 5)
    first = call(first_step, (ROWS, WIDE), 6 * 8 * ROWS * ROWS * WIDE, BLOCKS // 3, (V,) * 7 + (S,) * 2)
    second = call(second_step, (WIDE, ROWS), 6 * 8 * ROWS * ROWS * WIDE, BLOCKS // 3, (V,) * 8 + (S,) * 2)
    a, b, c, d = neighbours(start)
    own_part = own(start, a, b, *blocks)
    middle = first(own_part, c, d, *blocks, start, live, center, width)
    a, b, c, d = neighbours(middle)
    own_part = own(middle, a, b, *blocks)
    filtered = second(own_part, c, d, *blocks, middle, start, live, center, width)
    return jnp.transpose(filtered.reshape(ELEMS, BANDS, ROWS), (0, 2, 1))


def solution(mesh):
    inner = Mesh(
        mesh.devices.reshape(LAYERS, COLUMNS, CORES, FAR, NEAR // 2, 2), ELEM + BAND
    )
    return jax.shard_map(
        shards,
        mesh=inner,
        in_specs=(P(ELEM, BAND, None), P(BAND, None), P(ELEM), P(ELEM, None, None, None), P(), P()),
        out_specs=P(ELEM, None, BAND),
        check_vma=False,
    )
```

```python
import jax
import jax.numpy as jnp
from jax import lax
from jax.experimental import pallas as pl
from jax.experimental.pallas import tpu as pltpu
from jax.sharding import Mesh
from jax.sharding import PartitionSpec as P

LAYERS, COLUMNS, CORES = 4, 4, 2
FAR, LOW, NEAR = 4, 4, 8
ELEMS, ROWS, WIDE = 4, 160, 128
BANDS = 32
PIECE = 5
ELEM = ("layer", "column", "core")
RING = ("column", "core")
NEARS = ("z_lo", "y_hi")
BAND = ("z_hi",) + NEARS
F32, BF16 = jnp.float32, jnp.bfloat16


def call(kernel, out, flops, moved, spaces, scratch=(), kind=F32):
    several = isinstance(out[0], tuple)
    shapes = tuple(jax.ShapeDtypeStruct(o, kind) for o in (out if several else (out,)))
    specs = tuple(pl.BlockSpec(memory_space=pltpu.VMEM) for _ in shapes)
    return pl.pallas_call(
        kernel,
        out_shape=shapes if several else shapes[0],
        in_specs=[pl.BlockSpec(memory_space=s) for s in spaces],
        out_specs=specs if several else specs[0],
        scratch_shapes=scratch,
        compiler_params=pltpu.CompilerParams(vmem_limit_bytes=32 << 20),
        cost_estimate=pl.CostEstimate(flops=flops, bytes_accessed=moved, transcendentals=0),
    )


def split(v):
    high = v.astype(BF16)
    return high, (v - high.astype(F32)).astype(BF16)


def dot3(a, b):
    def dot(x, y):
        return jnp.dot(x, y, preferred_element_type=F32)

    return dot(a[0], b[0]) + (dot(a[0], b[1]) + dot(a[1], b[0]))


def lane_owner(shape):
    return lax.broadcasted_iota(jnp.int32, shape, len(shape) - 1) // BANDS


def by_owner(parts):
    owner = lane_owner(parts[0].shape)
    picked = parts[0]
    for e in range(1, ELEMS):
        picked = jnp.where(owner == e, parts[e], picked)
    return picked


def turned(v, by):
    by = by % ELEMS
    return pltpu.roll(v, by * BANDS, 1) if by else v


def alive(counts_ref):
    owner = lane_owner((ROWS, WIDE))
    row = lax.broadcasted_iota(jnp.int32, (ROWS, WIDE), 0)
    limit = jnp.full((ROWS, WIDE), counts_ref[0], jnp.int32)
    for e in range(1, ELEMS):
        limit = jnp.where(owner == e, counts_ref[e], limit)
    return row < limit


def cut_columns(orbitals_ref, rotation_ref, counts_ref, out_ref, mine_ref, live_ref):
    for far in range(FAR):
        lanes = pl.ds(pl.multiple_of(256 * far + 128 * lax.axis_index("core"), 128), 128)
        mine_ref[far] = rotation_ref[:, lanes]
    live_ref[...] = jnp.where(alive(counts_ref), 1.0, 0.0)
    first = lax.broadcasted_iota(jnp.int32, (ELEMS, WIDE), 1) < 64
    for i in range(PIECE):
        for low in range(LOW):
            half, odd = divmod(low, 2)
            for k in range(2):
                parts = [orbitals_ref[i, :, pl.ds(256 * far + 128 * half, 128)] for far in (2 * k, 2 * k + 1)]
                parts[1 - odd] = turned(parts[1 - odd], 2)
                out_ref[low, pl.ds(20 * k + ELEMS * i, ELEMS), :] = jnp.where(first, parts[0], parts[1])


def far_place(by):
    return lax.rem(lax.axis_index("z_hi") + by, FAR)


HALF = ROWS // 2
PASS = HALF + 32


def pack(rows_ref, mine_ref, other_ref, up_ref, down_ref, own_ref):
    for k in range(2):
        first, second = (down_ref, up_ref) if k else (up_ref, down_ref)
        for e in range(ELEMS):
            for low in range(LOW):
                for i in range(PIECE):
                    at = 20 * e + PIECE * low + i
                    row = rows_ref[low, pl.ds(20 * k + ELEMS * i + e, 1), :]
                    first[pl.ds(at, 1), :] = row
                    second[pl.ds(PASS + at, 1), :] = row
    lower = lax.axis_index("y_hi") == 0

    def slices(by):
        mine, other = mine_ref[far_place(by)], other_ref[far_place(by)]
        return jnp.where(lower, mine, other), jnp.where(lower, other, mine)

    up_ref[HALF:PASS, :], down_ref[HALF:PASS, :] = slices(2)
    tail = PASS + HALF
    up_ref[tail : tail + 32, :], up_ref[tail + 32 :, :] = slices(1)
    down_ref[tail : tail + 32, :], down_ref[tail + 32 :, :] = slices(3)
    own_ref[:32, :], own_ref[32:, :] = slices(0)


def collect(own_ref, below_ref, above_ref, passed_up_ref, passed_down_ref, out_ref):
    tail = PASS + HALF
    passed = jnp.concatenate([passed_up_ref[HALF:, :], passed_down_ref[HALF:, :]], axis=0)
    for by, piece in ((0, own_ref[...]), (3, below_ref[tail:, :]), (1, above_ref[tail:, :]), (2, passed)):
        out_ref[pl.ds(pl.multiple_of(64 * far_place(by), 64), 64), :] = piece


def rotate(
    up_ref, down_ref, mine_ref, other_ref, below_ref, above_ref, passed_up_ref, passed_down_ref, out_ref, sum_ref
):
    tail = PASS + HALF
    sides = [
        (0, up_ref[:HALF, :], down_ref[:HALF, :]),
        (3, below_ref[:HALF, :], below_ref[PASS:tail, :]),
        (1, above_ref[PASS:tail, :], above_ref[:HALF, :]),
        (2, passed_up_ref[:HALF, :], passed_down_ref[:HALF, :]),
    ]
    first = lax.axis_index("core") == 0
    mine, other = mine_ref[...], other_ref[...]
    halves = [split(jnp.where(first, mine, other)), split(jnp.where(first, other, mine))]
    for by, top, bottom in sides:
        rows = split(jnp.concatenate([top, bottom], axis=1))
        for half in range(2):
            sum_ref[half] = dot3(rows, halves[half])
        for near in range(NEAR):
            half, place = divmod(near, ELEMS)
            out_ref[near, pl.ds(20 * by, 20), :] = by_owner(
                [turned(sum_ref[half, pl.ds(20 * e, 20), :], e - place) for e in range(ELEMS)]
            )


def add_up(parts_ref, live_ref, out_ref, sum_ref, rows_ref):
    for share in range(2):
        total = parts_ref[share]
        for low in range(1, LOW):
            total = total + parts_ref[2 * low + share]
        sum_ref[share] = total
    for by in range(FAR):
        for share in range(2):
            for low in range(LOW):
                rows_ref[pl.ds(10 * low + PIECE * share, PIECE), :] = sum_ref[share, pl.ds(20 * by + PIECE * low, PIECE), :]
        at = pl.ds(pl.multiple_of(40 * far_place(by), 8), 40)
        out_ref[at, :] = jnp.where(live_ref[at, :] > 0.5, rows_ref[...], 0.0)


def split_blocks(hamiltonian_ref, high_ref, low_ref):
    for e in range(ELEMS):
        for slot in range(7):
            high_ref[e, slot], low_ref[e, slot] = split(hamiltonian_ref[e, slot])


def blocks_times(high_ref, low_ref, slots, fields):
    def dot(x, y):
        return jnp.dot(x, y, preferred_element_type=F32)

    fields = [split(f) for f in fields]
    pairs = [jnp.concatenate(f, axis=1) for f in fields]
    totals = []
    for e in range(ELEMS):
        wide = narrow = None
        for slot, field, pair in zip(slots, fields, pairs):
            first, second = dot(high_ref[e, slot], pair), dot(low_ref[e, slot], field[0])
            wide = first if wide is None else wide + first
            narrow = second if narrow is None else narrow + second
        totals.append(wide[:, :WIDE] + (wide[:, WIDE:] + narrow))
    return by_owner(totals)


def own_and_ring(field_ref, a_ref, b_ref, high_ref, low_ref, out_ref):
    field = field_ref[...]
    out_ref[...] = blocks_times(
        high_ref, low_ref, range(5), (field, turned(field, 1), turned(field, -1), a_ref[...], b_ref[...])
    )


def applied(own_ref, c_ref, d_ref, high_ref, low_ref, live_ref):
    total = own_ref[...] + blocks_times(high_ref, low_ref, (5, 6), (c_ref[...], d_ref[...]))
    return jnp.where(live_ref[...] > 0.5, total, 0.0)


def first_step(own_ref, c_ref, d_ref, high_ref, low_ref, start_ref, live_ref, center_ref, width_ref, out_ref):
    total = applied(own_ref, c_ref, d_ref, high_ref, low_ref, live_ref)
    out_ref[...] = (total - center_ref[0] * start_ref[...]) / width_ref[0]


def second_step(own_ref, c_ref, d_ref, high_ref, low_ref, middle_ref, start_ref, live_ref, center_ref, width_ref, out_ref):
    total = applied(own_ref, c_ref, d_ref, high_ref, low_ref, live_ref)
    filtered = 2.0 * (total - center_ref[0] * middle_ref[...]) / width_ref[0] - start_ref[...]
    out_ref[...] = jnp.transpose(filtered)


def neighbours(field):
    ring = COLUMNS * CORES
    return (
        lax.ppermute(field, RING, [(i, (i + 1) % ring) for i in range(ring)]),
        lax.ppermute(field, RING, [(i, (i - 1) % ring) for i in range(ring)]),
        lax.ppermute(field, "layer", [(i, i + 1) for i in range(LAYERS - 1)]),
        lax.ppermute(field, "layer", [(i + 1, i) for i in range(LAYERS - 1)]),
    )


def far_step(v, by):
    return lax.ppermute(v, "z_hi", [(i, (i + by) % FAR) for i in range(FAR)])


V, S = pltpu.VMEM, pltpu.SMEM
FIELD = ROWS * WIDE * 4
BLOCKS = ELEMS * 7 * ROWS * 256 * 4


def shards(orbitals, rotation, counts, hamiltonian, center, width):
    pieces = jnp.transpose(orbitals, (1, 0, 2))
    shapes = ((LOW, 2 * ELEMS * PIECE, WIDE), (FAR, 32, WIDE), (ROWS, WIDE))
    cut, mine, live = call(cut_columns, shapes, 0, 4 * FIELD, (V, V, S))(pieces, rotation, counts)
    other = lax.ppermute(mine, "y_hi", [(0, 1), (1, 0)])
    cut = lax.all_to_all(cut, "z_lo", split_axis=0, concat_axis=0, tiled=True)
    message = (2 * PASS + 32, WIDE)
    up, down, slices = call(pack, (message, message, (64, WIDE)), 0, 6 * FIELD, (V,) * 3)(cut, mine, other)
    above, below = far_step(down, -1), far_step(up, 1)
    passed_up, passed_down = far_step(below[:PASS], 1), far_step(above[:PASS], -1)
    blocks = call(split_blocks, (hamiltonian.shape,) * 2, 0, 2 * BLOCKS, (V,), (), BF16)(hamiltonian)
    slices, *blocks = lax.optimization_barrier((slices, *blocks))
    mine = call(collect, (256, WIDE), 0, 4 * FIELD, (V,) * 5)(slices, below, above, passed_up, passed_down)
    other = lax.ppermute(mine, "core", [(0, 1), (1, 0)])
    scratch = [V((2, HALF, WIDE), F32)]
    parts = call(rotate, (NEAR, HALF, WIDE), 6 * 320 * 256 * 256, 11 * FIELD, (V,) * 8, scratch)(
        up, down, mine, other, below, above, passed_up, passed_down
    )
    parts = lax.all_to_all(parts, NEARS, split_axis=0, concat_axis=0, tiled=True)
    scratch = [V((2, HALF, WIDE), F32), V((40, WIDE), F32)]
    start = call(add_up, (ROWS, WIDE), 0, 5 * FIELD, (V, V), scratch)(parts, live)

    own = call(own_and_ring, (ROWS, WIDE), 6 * 20 * ROWS * ROWS * WIDE, BLOCKS, (V,) * 5)
    first = call(first_step, (ROWS, WIDE), 6 * 8 * ROWS * ROWS * WIDE, BLOCKS // 3, (V,) * 7 + (S,) * 2)
    second = call(second_step, (WIDE, ROWS), 6 * 8 * ROWS * ROWS * WIDE, BLOCKS // 3, (V,) * 8 + (S,) * 2)
    a, b, c, d = neighbours(start)
    own_part = own(start, a, b, *blocks)
    middle = first(own_part, c, d, *blocks, start, live, center, width)
    a, b, c, d = neighbours(middle)
    own_part = own(middle, a, b, *blocks)
    filtered = second(own_part, c, d, *blocks, middle, start, live, center, width)
    return jnp.transpose(filtered.reshape(ELEMS, BANDS, ROWS), (0, 2, 1))


def solution(mesh):
    inner = Mesh(
        mesh.devices.reshape(LAYERS, COLUMNS, CORES, FAR, NEAR // 2, 2), ELEM + BAND
    )
    return jax.shard_map(
        shards,
        mesh=inner,
        in_specs=(P(ELEM, BAND, None), P(BAND, None), P(ELEM), P(ELEM, None, None, None), P(), P()),
        out_specs=P(ELEM, None, BAND),
        check_vma=False,
    )
```

```python
import jax
import jax.numpy as jnp
from jax import lax
from jax.experimental import pallas as pl
from jax.experimental.pallas import tpu as pltpu
from jax.sharding import Mesh
from jax.sharding import PartitionSpec as P

LAYERS, COLUMNS, CORES = 4, 4, 2
FAR, LOW, NEAR = 4, 4, 8
ELEMS, ROWS, WIDE = 4, 160, 128
BANDS = 32
PIECE = 5
ELEM = ("layer", "column", "core")
RING = ("column", "core")
NEARS = ("z_lo", "y_hi")
BAND = ("z_hi",) + NEARS
F32, BF16 = jnp.float32, jnp.bfloat16


def call(kernel, out, flops, moved, spaces, scratch=(), kind=F32):
    several = isinstance(out[0], tuple)
    shapes = tuple(jax.ShapeDtypeStruct(o, kind) for o in (out if several else (out,)))
    specs = tuple(pl.BlockSpec(memory_space=pltpu.VMEM) for _ in shapes)
    return pl.pallas_call(
        kernel,
        out_shape=shapes if several else shapes[0],
        in_specs=[pl.BlockSpec(memory_space=s) for s in spaces],
        out_specs=specs if several else specs[0],
        scratch_shapes=scratch,
        compiler_params=pltpu.CompilerParams(vmem_limit_bytes=32 << 20),
        cost_estimate=pl.CostEstimate(flops=flops, bytes_accessed=moved, transcendentals=0),
    )


def split(v):
    high = v.astype(BF16)
    return high, (v - high.astype(F32)).astype(BF16)


def dot3(a, b):
    def dot(x, y):
        return jnp.dot(x, y, preferred_element_type=F32)

    return dot(a[0], b[0]) + (dot(a[0], b[1]) + dot(a[1], b[0]))


def lane_owner(shape):
    return lax.broadcasted_iota(jnp.int32, shape, len(shape) - 1) // BANDS


def by_owner(parts):
    owner = lane_owner(parts[0].shape)
    picked = parts[0]
    for e in range(1, ELEMS):
        picked = jnp.where(owner == e, parts[e], picked)
    return picked


def turned(v, by):
    by = by % ELEMS
    return pltpu.roll(v, by * BANDS, 1) if by else v


def alive(counts_ref):
    owner = lane_owner((ROWS, WIDE))
    row = lax.broadcasted_iota(jnp.int32, (ROWS, WIDE), 0)
    limit = jnp.full((ROWS, WIDE), counts_ref[0], jnp.int32)
    for e in range(1, ELEMS):
        limit = jnp.where(owner == e, counts_ref[e], limit)
    return row < limit


def cut_rotation(rotation_ref, mine_ref):
    for far in range(FAR):
        lanes = pl.ds(pl.multiple_of(256 * far + 128 * lax.axis_index("core"), 128), 128)
        mine_ref[far] = rotation_ref[:, lanes]


def cut_columns(orbitals_ref, out_ref):
    first = lax.broadcasted_iota(jnp.int32, (ELEMS, WIDE), 1) < 64
    for i in range(PIECE):
        for low in range(LOW):
            half, odd = divmod(low, 2)
            for k in range(2):
                parts = [orbitals_ref[i, :, pl.ds(256 * far + 128 * half, 128)] for far in (2 * k, 2 * k + 1)]
                parts[1 - odd] = turned(parts[1 - odd], 2)
                out_ref[low, pl.ds(20 * k + ELEMS * i, ELEMS), :] = jnp.where(first, parts[0], parts[1])


def far_place(by):
    return lax.rem(lax.axis_index("z_hi") + by, FAR)


HALF = ROWS // 2
PASS = HALF + 32


def pack(rows_ref, mine_ref, other_ref, up_ref, down_ref, own_ref):
    for k in range(2):
        first, second = (down_ref, up_ref) if k else (up_ref, down_ref)
        for e in range(ELEMS):
            for low in range(LOW):
                for i in range(PIECE):
                    at = 20 * e + PIECE * low + i
                    row = rows_ref[low, pl.ds(20 * k + ELEMS * i + e, 1), :]
                    first[pl.ds(at, 1), :] = row
                    second[pl.ds(PASS + at, 1), :] = row
    lower = lax.axis_index("y_hi") == 0

    def slices(by):
        mine, other = mine_ref[far_place(by)], other_ref[far_place(by)]
        return jnp.where(lower, mine, other), jnp.where(lower, other, mine)

    up_ref[HALF:PASS, :], down_ref[HALF:PASS, :] = slices(2)
    tail = PASS + HALF
    up_ref[tail : tail + 32, :], up_ref[tail + 32 :, :] = slices(1)
    down_ref[tail : tail + 32, :], down_ref[tail + 32 :, :] = slices(3)
    own_ref[:32, :], own_ref[32:, :] = slices(0)


def collect(own_ref, below_ref, above_ref, passed_up_ref, passed_down_ref, out_ref):
    tail = PASS + HALF
    passed = jnp.concatenate([passed_up_ref[HALF:, :], passed_down_ref[HALF:, :]], axis=0)
    for by, piece in ((0, own_ref[...]), (3, below_ref[tail:, :]), (1, above_ref[tail:, :]), (2, passed)):
        out_ref[pl.ds(pl.multiple_of(64 * far_place(by), 64), 64), :] = piece


def rotate(
    up_ref, down_ref, mine_ref, other_ref, below_ref, above_ref, passed_up_ref, passed_down_ref, out_ref, sum_ref
):
    tail = PASS + HALF
    sides = [
        (0, up_ref[:HALF, :], down_ref[:HALF, :]),
        (3, below_ref[:HALF, :], below_ref[PASS:tail, :]),
        (1, above_ref[PASS:tail, :], above_ref[:HALF, :]),
        (2, passed_up_ref[:HALF, :], passed_down_ref[:HALF, :]),
    ]
    first = lax.axis_index("core") == 0
    mine, other = mine_ref[...], other_ref[...]
    halves = [split(jnp.where(first, mine, other)), split(jnp.where(first, other, mine))]
    for by, top, bottom in sides:
        rows = split(jnp.concatenate([top, bottom], axis=1))
        for half in range(2):
            sum_ref[half] = dot3(rows, halves[half])
        for near in range(NEAR):
            half, place = divmod(near, ELEMS)
            out_ref[near, pl.ds(20 * by, 20), :] = by_owner(
                [turned(sum_ref[half, pl.ds(20 * e, 20), :], e - place) for e in range(ELEMS)]
            )


def add_up(parts_ref, live_ref, out_ref, sum_ref, rows_ref):
    for share in range(2):
        total = parts_ref[share]
        for low in range(1, LOW):
            total = total + parts_ref[2 * low + share]
        sum_ref[share] = total
    for by in range(FAR):
        for share in range(2):
            for low in range(LOW):
                rows_ref[pl.ds(10 * low + PIECE * share, PIECE), :] = sum_ref[share, pl.ds(20 * by + PIECE * low, PIECE), :]
        at = pl.ds(pl.multiple_of(40 * far_place(by), 8), 40)
        out_ref[at, :] = jnp.where(live_ref[at, :].astype(F32) > 0.5, rows_ref[...], 0.0)


def split_blocks(hamiltonian_ref, counts_ref, high_ref, low_ref, live_ref):
    live_ref[...] = jnp.where(alive(counts_ref), 1.0, 0.0).astype(BF16)
    for e in range(ELEMS):
        for slot in range(7):
            high_ref[e, slot], low_ref[e, slot] = split(hamiltonian_ref[e, slot])


def blocks_times(high_ref, low_ref, slots, fields):
    def dot(x, y):
        return jnp.dot(x, y, preferred_element_type=F32)

    fields = [split(f) for f in fields]
    pairs = [jnp.concatenate(f, axis=1) for f in fields]
    totals = []
    for e in range(ELEMS):
        wide = narrow = None
        for slot, field, pair in zip(slots, fields, pairs):
            first, second = dot(high_ref[e, slot], pair), dot(low_ref[e, slot], field[0])
            wide = first if wide is None else wide + first
            narrow = second if narrow is None else narrow + second
        totals.append(wide[:, :WIDE] + (wide[:, WIDE:] + narrow))
    return by_owner(totals)


def own_and_ring(field_ref, a_ref, b_ref, high_ref, low_ref, out_ref):
    field = field_ref[...]
    out_ref[...] = blocks_times(
        high_ref, low_ref, range(5), (field, turned(field, 1), turned(field, -1), a_ref[...], b_ref[...])
    )


def applied(own_ref, c_ref, d_ref, high_ref, low_ref, live_ref):
    total = own_ref[...] + blocks_times(high_ref, low_ref, (5, 6), (c_ref[...], d_ref[...]))
    return jnp.where(live_ref[...].astype(F32) > 0.5, total, 0.0)


def first_step(own_ref, c_ref, d_ref, high_ref, low_ref, start_ref, live_ref, center_ref, width_ref, out_ref):
    total = applied(own_ref, c_ref, d_ref, high_ref, low_ref, live_ref)
    out_ref[...] = (total - center_ref[0] * start_ref[...]) / width_ref[0]


def second_step(own_ref, c_ref, d_ref, high_ref, low_ref, middle_ref, start_ref, live_ref, center_ref, width_ref, out_ref):
    total = applied(own_ref, c_ref, d_ref, high_ref, low_ref, live_ref)
    filtered = 2.0 * (total - center_ref[0] * middle_ref[...]) / width_ref[0] - start_ref[...]
    out_ref[...] = jnp.transpose(filtered)


def neighbours(field):
    ring = COLUMNS * CORES
    return (
        lax.ppermute(field, RING, [(i, (i + 1) % ring) for i in range(ring)]),
        lax.ppermute(field, RING, [(i, (i - 1) % ring) for i in range(ring)]),
        lax.ppermute(field, "layer", [(i, i + 1) for i in range(LAYERS - 1)]),
        lax.ppermute(field, "layer", [(i + 1, i) for i in range(LAYERS - 1)]),
    )


def far_step(v, by):
    return lax.ppermute(v, "z_hi", [(i, (i + by) % FAR) for i in range(FAR)])


V, S = pltpu.VMEM, pltpu.SMEM
FIELD = ROWS * WIDE * 4
BLOCKS = ELEMS * 7 * ROWS * 256 * 4


def shards(orbitals, rotation, counts, hamiltonian, center, width):
    pieces = jnp.transpose(orbitals, (1, 0, 2))
    mine = call(cut_rotation, (FAR, 32, WIDE), 0, 2 * FIELD, (V,))(rotation)
    other = lax.ppermute(mine, "y_hi", [(0, 1), (1, 0)])
    cut = call(cut_columns, (LOW, 2 * ELEMS * PIECE, WIDE), 0, 2 * FIELD, (V,))(pieces)
    cut = lax.all_to_all(cut, "z_lo", split_axis=0, concat_axis=0, tiled=True)
    message = (2 * PASS + 32, WIDE)
    up, down, slices = call(pack, (message, message, (64, WIDE)), 0, 6 * FIELD, (V,) * 3)(cut, mine, other)
    above, below = far_step(down, -1), far_step(up, 1)
    shapes = (hamiltonian.shape, hamiltonian.shape, (ROWS, WIDE))
    blocks = call(split_blocks, shapes, 0, 2 * BLOCKS, (V, S), (), BF16)(hamiltonian, counts)
    below, *blocks, live = lax.optimization_barrier((below, *blocks))
    passed_up, passed_down = far_step(below[:PASS], 1), far_step(above[:PASS], -1)
    mine = call(collect, (256, WIDE), 0, 4 * FIELD, (V,) * 5)(slices, below, above, passed_up, passed_down)
    other = lax.ppermute(mine, "core", [(0, 1), (1, 0)])
    scratch = [V((2, HALF, WIDE), F32)]
    parts = call(rotate, (NEAR, HALF, WIDE), 6 * 320 * 256 * 256, 11 * FIELD, (V,) * 8, scratch)(
        up, down, mine, other, below, above, passed_up, passed_down
    )
    parts = lax.all_to_all(parts, NEARS, split_axis=0, concat_axis=0, tiled=True)
    scratch = [V((2, HALF, WIDE), F32), V((40, WIDE), F32)]
    start = call(add_up, (ROWS, WIDE), 0, 5 * FIELD, (V, V), scratch)(parts, live)

    own = call(own_and_ring, (ROWS, WIDE), 6 * 20 * ROWS * ROWS * WIDE, BLOCKS, (V,) * 5)
    first = call(first_step, (ROWS, WIDE), 6 * 8 * ROWS * ROWS * WIDE, BLOCKS // 3, (V,) * 7 + (S,) * 2)
    second = call(second_step, (WIDE, ROWS), 6 * 8 * ROWS * ROWS * WIDE, BLOCKS // 3, (V,) * 8 + (S,) * 2)
    a, b, c, d = neighbours(start)
    own_part = own(start, a, b, *blocks)
    middle = first(own_part, c, d, *blocks, start, live, center, width)
    a, b, c, d = neighbours(middle)
    own_part = own(middle, a, b, *blocks)
    filtered = second(own_part, c, d, *blocks, middle, start, live, center, width)
    return jnp.transpose(filtered.reshape(ELEMS, BANDS, ROWS), (0, 2, 1))


def solution(mesh):
    inner = Mesh(
        mesh.devices.reshape(LAYERS, COLUMNS, CORES, FAR, NEAR // 2, 2), ELEM + BAND
    )
    return jax.shard_map(
        shards,
        mesh=inner,
        in_specs=(P(ELEM, BAND, None), P(BAND, None), P(ELEM), P(ELEM, None, None, None), P(), P()),
        out_specs=P(ELEM, None, BAND),
        check_vma=False,
    )
```

```python
import jax
import jax.numpy as jnp
from jax import lax
from jax.experimental import pallas as pl
from jax.experimental.pallas import tpu as pltpu
from jax.sharding import Mesh
from jax.sharding import PartitionSpec as P

LAYERS, COLUMNS, CORES = 4, 4, 2
FAR, LOW, NEAR = 4, 4, 8
ELEMS, ROWS, WIDE = 4, 160, 128
BANDS = 32
PIECE = 5
ELEM = ("layer", "column", "core")
RING = ("column", "core")
NEARS = ("z_lo", "y_hi")
BAND = ("z_hi",) + NEARS
F32, BF16 = jnp.float32, jnp.bfloat16


def call(kernel, out, flops, moved, spaces, scratch=(), kind=F32):
    several = isinstance(out[0], tuple)
    shapes = tuple(jax.ShapeDtypeStruct(o, kind) for o in (out if several else (out,)))
    specs = tuple(pl.BlockSpec(memory_space=pltpu.VMEM) for _ in shapes)
    return pl.pallas_call(
        kernel,
        out_shape=shapes if several else shapes[0],
        in_specs=[pl.BlockSpec(memory_space=s) for s in spaces],
        out_specs=specs if several else specs[0],
        scratch_shapes=scratch,
        compiler_params=pltpu.CompilerParams(vmem_limit_bytes=32 << 20),
        cost_estimate=pl.CostEstimate(flops=flops, bytes_accessed=moved, transcendentals=0),
    )


def split(v):
    high = v.astype(BF16)
    return high, (v - high.astype(F32)).astype(BF16)


def dot3(a, b):
    def dot(x, y):
        return jnp.dot(x, y, preferred_element_type=F32)

    return dot(a[0], b[0]) + (dot(a[0], b[1]) + dot(a[1], b[0]))


def lane_owner(shape):
    return lax.broadcasted_iota(jnp.int32, shape, len(shape) - 1) // BANDS


def by_owner(parts):
    owner = lane_owner(parts[0].shape)
    picked = parts[0]
    for e in range(1, ELEMS):
        picked = jnp.where(owner == e, parts[e], picked)
    return picked


def turned(v, by):
    by = by % ELEMS
    return pltpu.roll(v, by * BANDS, 1) if by else v


def alive(counts_ref):
    owner = lane_owner((ROWS, WIDE))
    row = lax.broadcasted_iota(jnp.int32, (ROWS, WIDE), 0)
    limit = jnp.full((ROWS, WIDE), counts_ref[0], jnp.int32)
    for e in range(1, ELEMS):
        limit = jnp.where(owner == e, counts_ref[e], limit)
    return row < limit


def cut_rotation(rotation_ref, mine_ref):
    for far in range(FAR):
        lanes = pl.ds(pl.multiple_of(256 * far + 128 * lax.axis_index("core"), 128), 128)
        mine_ref[far] = rotation_ref[:, lanes]


def cut_columns(orbitals_ref, out_ref):
    first = lax.broadcasted_iota(jnp.int32, (ELEMS, WIDE), 1) < 64
    for i in range(PIECE):
        for low in range(LOW):
            half, odd = divmod(low, 2)
            for k in range(2):
                parts = [orbitals_ref[i, :, pl.ds(256 * far + 128 * half, 128)] for far in (2 * k, 2 * k + 1)]
                parts[1 - odd] = turned(parts[1 - odd], 2)
                out_ref[low, pl.ds(20 * k + ELEMS * i, ELEMS), :] = jnp.where(first, parts[0], parts[1])


def far_place(by):
    return lax.rem(lax.axis_index("z_hi") + by, FAR)


HALF = ROWS // 2
PASS = HALF + 32


def by_parity(body, first, second, *relayed):
    even = lax.rem(lax.axis_index("z_hi"), 2) == 0
    pl.when(even)(lambda: body(first, second, *relayed))
    pl.when(jnp.logical_not(even))(lambda: body(second, first, *reversed(relayed)))


def pack(rows_ref, mine_ref, other_ref, first_ref, second_ref, own_ref):
    by_parity(lambda up, down: pack_into(rows_ref, mine_ref, other_ref, up, down, own_ref), first_ref, second_ref)


def pack_into(rows_ref, mine_ref, other_ref, up_ref, down_ref, own_ref):
    for k in range(2):
        first, second = (down_ref, up_ref) if k else (up_ref, down_ref)
        for e in range(ELEMS):
            for low in range(LOW):
                for i in range(PIECE):
                    at = 20 * e + PIECE * low + i
                    row = rows_ref[low, pl.ds(20 * k + ELEMS * i + e, 1), :]
                    first[pl.ds(at, 1), :] = row
                    second[pl.ds(PASS + at, 1), :] = row
    lower = lax.axis_index("y_hi") == 0

    def slices(by):
        mine, other = mine_ref[far_place(by)], other_ref[far_place(by)]
        return jnp.where(lower, mine, other), jnp.where(lower, other, mine)

    up_ref[HALF:PASS, :], down_ref[HALF:PASS, :] = slices(2)
    tail = PASS + HALF
    up_ref[tail : tail + 32, :], up_ref[tail + 32 :, :] = slices(1)
    down_ref[tail : tail + 32, :], down_ref[tail + 32 :, :] = slices(3)
    own_ref[:32, :], own_ref[32:, :] = slices(0)


def collect(own_ref, near_ref, next_ref, passed_ref, last_ref, out_ref):
    def body(above, below, passed_up, passed_down):
        collect_from(own_ref, below, above, passed_up, passed_down, out_ref)

    by_parity(body, near_ref, next_ref, passed_ref, last_ref)


def collect_from(own_ref, below_ref, above_ref, passed_up_ref, passed_down_ref, out_ref):
    tail = PASS + HALF
    passed = jnp.concatenate([passed_up_ref[HALF:, :], passed_down_ref[HALF:, :]], axis=0)
    for by, piece in ((0, own_ref[...]), (3, below_ref[tail:, :]), (1, above_ref[tail:, :]), (2, passed)):
        out_ref[pl.ds(pl.multiple_of(64 * far_place(by), 64), 64), :] = piece


def rotate(
    first_ref, second_ref, mine_ref, other_ref, near_ref, next_ref, passed_ref, last_ref, out_ref, sum_ref
):
    def body(up, down, above, passed_up, passed_down, below):
        rotate_from(up, down, mine_ref, other_ref, below, above, passed_up, passed_down, out_ref, sum_ref)

    by_parity(body, first_ref, second_ref, near_ref, passed_ref, last_ref, next_ref)


def rotate_from(
    up_ref, down_ref, mine_ref, other_ref, below_ref, above_ref, passed_up_ref, passed_down_ref, out_ref, sum_ref
):
    tail = PASS + HALF
    sides = [
        (0, up_ref[:HALF, :], down_ref[:HALF, :]),
        (3, below_ref[:HALF, :], below_ref[PASS:tail, :]),
        (1, above_ref[PASS:tail, :], above_ref[:HALF, :]),
        (2, passed_up_ref[:HALF, :], passed_down_ref[:HALF, :]),
    ]
    first = lax.axis_index("core") == 0
    mine, other = mine_ref[...], other_ref[...]
    halves = [split(jnp.where(first, mine, other)), split(jnp.where(first, other, mine))]
    for by, top, bottom in sides:
        rows = split(jnp.concatenate([top, bottom], axis=1))
        for half in range(2):
            sum_ref[half] = dot3(rows, halves[half])
        for near in range(NEAR):
            half, place = divmod(near, ELEMS)
            out_ref[near, pl.ds(20 * by, 20), :] = by_owner(
                [turned(sum_ref[half, pl.ds(20 * e, 20), :], e - place) for e in range(ELEMS)]
            )


def add_up(parts_ref, live_ref, out_ref, sum_ref, rows_ref):
    for share in range(2):
        total = parts_ref[share]
        for low in range(1, LOW):
            total = total + parts_ref[2 * low + share]
        sum_ref[share] = total
    for by in range(FAR):
        for share in range(2):
            for low in range(LOW):
                rows_ref[pl.ds(10 * low + PIECE * share, PIECE), :] = sum_ref[share, pl.ds(20 * by + PIECE * low, PIECE), :]
        at = pl.ds(pl.multiple_of(40 * far_place(by), 8), 40)
        out_ref[at, :] = jnp.where(live_ref[at, :].astype(F32) > 0.5, rows_ref[...], 0.0)


def split_blocks(hamiltonian_ref, counts_ref, high_ref, low_ref, live_ref):
    live_ref[...] = jnp.where(alive(counts_ref), 1.0, 0.0).astype(BF16)
    for e in range(ELEMS):
        for slot in range(7):
            high_ref[e, slot], low_ref[e, slot] = split(hamiltonian_ref[e, slot])


def blocks_times(high_ref, low_ref, slots, fields):
    def dot(x, y):
        return jnp.dot(x, y, preferred_element_type=F32)

    fields = [split(f) for f in fields]
    pairs = [jnp.concatenate(f, axis=1) for f in fields]
    totals = []
    for e in range(ELEMS):
        wide = narrow = None
        for slot, field, pair in zip(slots, fields, pairs):
            first, second = dot(high_ref[e, slot], pair), dot(low_ref[e, slot], field[0])
            wide = first if wide is None else wide + first
            narrow = second if narrow is None else narrow + second
        totals.append(wide[:, :WIDE] + (wide[:, WIDE:] + narrow))
    return by_owner(totals)


def own_and_layers(field_ref, a_ref, b_ref, high_ref, low_ref, out_ref):
    field = field_ref[...]
    out_ref[...] = blocks_times(
        high_ref, low_ref, (0, 1, 2, 5, 6), (field, turned(field, 1), turned(field, -1), a_ref[...], b_ref[...])
    )


def applied(own_ref, c_ref, d_ref, high_ref, low_ref, live_ref):
    total = own_ref[...] + blocks_times(high_ref, low_ref, (3, 4), (c_ref[...], d_ref[...]))
    return jnp.where(live_ref[...].astype(F32) > 0.5, total, 0.0)


def first_step(own_ref, c_ref, d_ref, high_ref, low_ref, start_ref, live_ref, center_ref, width_ref, out_ref):
    total = applied(own_ref, c_ref, d_ref, high_ref, low_ref, live_ref)
    out_ref[...] = (total - center_ref[0] * start_ref[...]) / width_ref[0]


def second_step(own_ref, c_ref, d_ref, high_ref, low_ref, middle_ref, start_ref, live_ref, center_ref, width_ref, out_ref):
    total = applied(own_ref, c_ref, d_ref, high_ref, low_ref, live_ref)
    filtered = 2.0 * (total - center_ref[0] * middle_ref[...]) / width_ref[0] - start_ref[...]
    out_ref[...] = jnp.transpose(filtered)


def neighbours(field):
    ring = COLUMNS * CORES
    return (
        lax.ppermute(field, RING, [(i, (i + 1) % ring) for i in range(ring)]),
        lax.ppermute(field, RING, [(i, (i - 1) % ring) for i in range(ring)]),
        lax.ppermute(field, "layer", [(i, i + 1) for i in range(LAYERS - 1)]),
        lax.ppermute(field, "layer", [(i + 1, i) for i in range(LAYERS - 1)]),
    )


def swapped(v, start):
    pairs = [(i % FAR, (i + 1) % FAR) for i in range(start, FAR, 2)]
    return lax.ppermute(v, "z_hi", pairs + [(b, a) for a, b in pairs])


V, S = pltpu.VMEM, pltpu.SMEM
FIELD = ROWS * WIDE * 4
BLOCKS = ELEMS * 7 * ROWS * 256 * 4


def shards(orbitals, rotation, counts, hamiltonian, center, width):
    pieces = jnp.transpose(orbitals, (1, 0, 2))
    mine = call(cut_rotation, (FAR, 32, WIDE), 0, 2 * FIELD, (V,))(rotation)
    other = lax.ppermute(mine, "y_hi", [(0, 1), (1, 0)])
    cut = call(cut_columns, (LOW, 2 * ELEMS * PIECE, WIDE), 0, 2 * FIELD, (V,))(pieces)
    cut = lax.all_to_all(cut, "z_lo", split_axis=0, concat_axis=0, tiled=True)
    message = (2 * PASS + 32, WIDE)
    first, second, slices = call(pack, (message, message, (64, WIDE)), 0, 6 * FIELD, (V,) * 3)(cut, mine, other)
    near, after = swapped(first, 0), swapped(second, 1)
    shapes = (hamiltonian.shape, hamiltonian.shape, (ROWS, WIDE))
    blocks = call(split_blocks, shapes, 0, 2 * BLOCKS, (V, S), (), BF16)(hamiltonian, counts)
    near, *blocks, live = lax.optimization_barrier((near, *blocks))
    passed, last = swapped(near[:PASS], 1), swapped(after[:PASS], 0)
    mine = call(collect, (256, WIDE), 0, 4 * FIELD, (V,) * 5)(slices, near, after, passed, last)
    other = lax.ppermute(mine, "core", [(0, 1), (1, 0)])
    scratch = [V((2, HALF, WIDE), F32)]
    parts = call(rotate, (NEAR, HALF, WIDE), 6 * 320 * 256 * 256, 11 * FIELD, (V,) * 8, scratch)(
        first, second, mine, other, near, after, passed, last
    )
    parts = lax.all_to_all(parts, NEARS, split_axis=0, concat_axis=0, tiled=True)
    scratch = [V((2, HALF, WIDE), F32), V((40, WIDE), F32)]
    start = call(add_up, (ROWS, WIDE), 0, 5 * FIELD, (V, V), scratch)(parts, live)

    own = call(own_and_layers, (ROWS, WIDE), 6 * 20 * ROWS * ROWS * WIDE, BLOCKS, (V,) * 5)
    first = call(first_step, (ROWS, WIDE), 6 * 8 * ROWS * ROWS * WIDE, BLOCKS // 3, (V,) * 7 + (S,) * 2)
    second = call(second_step, (WIDE, ROWS), 6 * 8 * ROWS * ROWS * WIDE, BLOCKS // 3, (V,) * 8 + (S,) * 2)
    c, d, a, b = neighbours(start)
    own_part = own(start, a, b, *blocks)
    middle = first(own_part, c, d, *blocks, start, live, center, width)
    c, d, a, b = neighbours(middle)
    own_part = own(middle, a, b, *blocks)
    filtered = second(own_part, c, d, *blocks, middle, start, live, center, width)
    return jnp.transpose(filtered.reshape(ELEMS, BANDS, ROWS), (0, 2, 1))


def solution(mesh):
    inner = Mesh(
        mesh.devices.reshape(LAYERS, COLUMNS, CORES, FAR, NEAR // 2, 2), ELEM + BAND
    )
    return jax.shard_map(
        shards,
        mesh=inner,
        in_specs=(P(ELEM, BAND, None), P(BAND, None), P(ELEM), P(ELEM, None, None, None), P(), P()),
        out_specs=P(ELEM, None, BAND),
        check_vma=False,
    )
```

```python
import jax
import jax.numpy as jnp
from jax import lax
from jax.experimental import pallas as pl
from jax.experimental.pallas import tpu as pltpu
from jax.sharding import Mesh
from jax.sharding import PartitionSpec as P

LAYERS, COLUMNS, CORES = 4, 4, 2
FAR, LOW, NEAR = 4, 4, 8
ELEMS, ROWS, WIDE = 4, 160, 128
BANDS = 32
PIECE = 5
ELEM = ("layer", "column", "core")
RING = ("column", "core")
NEARS = ("z_lo", "y_hi")
BAND = ("z_hi",) + NEARS
F32, BF16 = jnp.float32, jnp.bfloat16


def call(kernel, out, flops, moved, spaces, scratch=(), kind=F32):
    several = isinstance(out[0], tuple)
    shapes = tuple(jax.ShapeDtypeStruct(o, kind) for o in (out if several else (out,)))
    specs = tuple(pl.BlockSpec(memory_space=pltpu.VMEM) for _ in shapes)
    return pl.pallas_call(
        kernel,
        out_shape=shapes if several else shapes[0],
        in_specs=[pl.BlockSpec(memory_space=s) for s in spaces],
        out_specs=specs if several else specs[0],
        scratch_shapes=scratch,
        compiler_params=pltpu.CompilerParams(vmem_limit_bytes=32 << 20),
        cost_estimate=pl.CostEstimate(flops=flops, bytes_accessed=moved, transcendentals=0),
    )


def split(v):
    high = v.astype(BF16)
    return high, (v - high.astype(F32)).astype(BF16)


def dot3(a, b):
    def dot(x, y):
        return jnp.dot(x, y, preferred_element_type=F32)

    return dot(a[0], b[0]) + (dot(a[0], b[1]) + dot(a[1], b[0]))


def lane_owner(shape):
    return lax.broadcasted_iota(jnp.int32, shape, len(shape) - 1) // BANDS


def by_owner(parts):
    owner = lane_owner(parts[0].shape)
    picked = parts[0]
    for e in range(1, ELEMS):
        picked = jnp.where(owner == e, parts[e], picked)
    return picked


def turned(v, by):
    by = by % ELEMS
    return pltpu.roll(v, by * BANDS, 1) if by else v


def alive(counts_ref):
    owner = lane_owner((ROWS, WIDE))
    row = lax.broadcasted_iota(jnp.int32, (ROWS, WIDE), 0)
    limit = jnp.full((ROWS, WIDE), counts_ref[0], jnp.int32)
    for e in range(1, ELEMS):
        limit = jnp.where(owner == e, counts_ref[e], limit)
    return row < limit


def cut_rotation(rotation_ref, mine_ref):
    for far in range(FAR):
        lanes = pl.ds(pl.multiple_of(256 * far + 128 * lax.axis_index("core"), 128), 128)
        mine_ref[0, far] = mine_ref[1, far] = rotation_ref[:, lanes]


def low_place(by):
    return lax.rem(lax.axis_index("z_lo") + by, LOW)


def cut_columns(orbitals_ref, *out_refs):
    first = lax.broadcasted_iota(jnp.int32, (ELEMS, WIDE), 1) < 64
    for by, out_ref in enumerate(out_refs):
        low = low_place(by)
        odd = jnp.full((ELEMS, WIDE), lax.rem(low, 2), jnp.int32) == 1
        for i in range(PIECE):
            for k in range(2):
                parts = []
                for far in (2 * k, 2 * k + 1):
                    lanes = pl.ds(pl.multiple_of(256 * far + 128 * lax.div(low, 2), 128), 128)
                    parts.append(orbitals_ref[i, :, lanes])
                even_form = jnp.where(first, parts[0], turned(parts[1], 2))
                odd_form = jnp.where(first, turned(parts[0], 2), parts[1])
                out_ref[pl.ds(20 * k + ELEMS * i, ELEMS), :] = jnp.where(odd, odd_form, even_form)


def far_place(by):
    return lax.rem(lax.axis_index("z_hi") + by, FAR)


HALF = ROWS // 2
PASS = HALF + 32


def pack(rows_0, rows_1, rows_2, rows_3, both_ref, up_ref, down_ref, own_ref):
    for k in range(2):
        first, second = (down_ref, up_ref) if k else (up_ref, down_ref)
        for e in range(ELEMS):
            for by, rows_ref in enumerate((rows_0, rows_1, rows_2, rows_3)):
                for i in range(PIECE):
                    at = 20 * e + PIECE * low_place(LOW - by) + i
                    row = rows_ref[pl.ds(20 * k + ELEMS * i + e, 1), :]
                    first[pl.ds(at, 1), :] = row
                    second[pl.ds(PASS + at, 1), :] = row
    def slices(by):
        return both_ref[0, far_place(by)], both_ref[1, far_place(by)]

    up_ref[HALF:PASS, :], down_ref[HALF:PASS, :] = slices(2)
    tail = PASS + HALF
    up_ref[tail : tail + 32, :], up_ref[tail + 32 :, :] = slices(1)
    down_ref[tail : tail + 32, :], down_ref[tail + 32 :, :] = slices(3)
    own_ref[:32, :], own_ref[32:, :] = slices(0)


def collect(own_ref, below_ref, above_ref, passed_up_ref, passed_down_ref, out_ref):
    tail = PASS + HALF
    passed = jnp.concatenate([passed_up_ref[HALF:, :], passed_down_ref[HALF:, :]], axis=0)
    for by, piece in ((0, own_ref[...]), (3, below_ref[tail:, :]), (1, above_ref[tail:, :]), (2, passed)):
        out_ref[pl.ds(pl.multiple_of(64 * far_place(by), 64), 64), :] = piece


def rotate(
    up_ref, down_ref, mine_ref, other_ref, below_ref, above_ref, passed_up_ref, passed_down_ref, out_ref, sum_ref
):
    tail = PASS + HALF
    sides = [
        (0, up_ref[:HALF, :], down_ref[:HALF, :]),
        (3, below_ref[:HALF, :], below_ref[PASS:tail, :]),
        (1, above_ref[PASS:tail, :], above_ref[:HALF, :]),
        (2, passed_up_ref[:HALF, :], passed_down_ref[:HALF, :]),
    ]
    first = lax.axis_index("core") == 0
    mine, other = mine_ref[...], other_ref[...]
    halves = [split(jnp.where(first, mine, other)), split(jnp.where(first, other, mine))]
    for by, top, bottom in sides:
        rows = split(jnp.concatenate([top, bottom], axis=1))
        for half in range(2):
            sum_ref[half] = dot3(rows, halves[half])
        for near in range(NEAR):
            half, place = divmod(near, ELEMS)
            out_ref[near, pl.ds(20 * by, 20), :] = by_owner(
                [turned(sum_ref[half, pl.ds(20 * e, 20), :], e - place) for e in range(ELEMS)]
            )


def add_up(parts_ref, live_ref, out_ref, sum_ref, rows_ref):
    for share in range(2):
        total = parts_ref[share]
        for low in range(1, LOW):
            total = total + parts_ref[2 * low + share]
        sum_ref[share] = total
    for by in range(FAR):
        for share in range(2):
            for low in range(LOW):
                rows_ref[pl.ds(10 * low + PIECE * share, PIECE), :] = sum_ref[share, pl.ds(20 * by + PIECE * low, PIECE), :]
        at = pl.ds(pl.multiple_of(40 * far_place(by), 8), 40)
        out_ref[at, :] = jnp.where(live_ref[at, :].astype(F32) > 0.5, rows_ref[...], 0.0)


def split_blocks(hamiltonian_ref, counts_ref, high_ref, low_ref, live_ref):
    live_ref[...] = jnp.where(alive(counts_ref), 1.0, 0.0).astype(BF16)
    for e in range(ELEMS):
        for slot in range(7):
            high_ref[e, slot], low_ref[e, slot] = split(hamiltonian_ref[e, slot])


def blocks_times(high_ref, low_ref, slots, fields):
    def dot(x, y):
        return jnp.dot(x, y, preferred_element_type=F32)

    fields = [split(f) for f in fields]
    pairs = [jnp.concatenate(f, axis=1) for f in fields]
    totals = []
    for e in range(ELEMS):
        wide = narrow = None
        for slot, field, pair in zip(slots, fields, pairs):
            first, second = dot(high_ref[e, slot], pair), dot(low_ref[e, slot], field[0])
            wide = first if wide is None else wide + first
            narrow = second if narrow is None else narrow + second
        totals.append(wide[:, :WIDE] + (wide[:, WIDE:] + narrow))
    return by_owner(totals)


def own_and_ring(field_ref, a_ref, b_ref, high_ref, low_ref, out_ref):
    field = field_ref[...]
    out_ref[...] = blocks_times(
        high_ref, low_ref, range(5), (field, turned(field, 1), turned(field, -1), a_ref[...], b_ref[...])
    )


def applied(own_ref, c_ref, d_ref, high_ref, low_ref, live_ref):
    total = own_ref[...] + blocks_times(high_ref, low_ref, (5, 6), (c_ref[...], d_ref[...]))
    return jnp.where(live_ref[...].astype(F32) > 0.5, total, 0.0)


def first_step(own_ref, c_ref, d_ref, high_ref, low_ref, start_ref, live_ref, center_ref, width_ref, out_ref):
    total = applied(own_ref, c_ref, d_ref, high_ref, low_ref, live_ref)
    out_ref[...] = (total - center_ref[0] * start_ref[...]) / width_ref[0]


def second_step(own_ref, c_ref, d_ref, high_ref, low_ref, middle_ref, start_ref, live_ref, center_ref, width_ref, out_ref):
    total = applied(own_ref, c_ref, d_ref, high_ref, low_ref, live_ref)
    filtered = 2.0 * (total - center_ref[0] * middle_ref[...]) / width_ref[0] - start_ref[...]
    out_ref[...] = jnp.transpose(filtered)


def neighbours(field):
    ring = COLUMNS * CORES
    return (
        lax.ppermute(field, RING, [(i, (i + 1) % ring) for i in range(ring)]),
        lax.ppermute(field, RING, [(i, (i - 1) % ring) for i in range(ring)]),
        lax.ppermute(field, "layer", [(i, i + 1) for i in range(LAYERS - 1)]),
        lax.ppermute(field, "layer", [(i + 1, i) for i in range(LAYERS - 1)]),
    )


def far_step(v, by):
    return lax.ppermute(v, "z_hi", [(i, (i + by) % FAR) for i in range(FAR)])


V, S = pltpu.VMEM, pltpu.SMEM
FIELD = ROWS * WIDE * 4
BLOCKS = ELEMS * 7 * ROWS * 256 * 4


def shards(orbitals, rotation, counts, hamiltonian, center, width):
    pieces = jnp.transpose(orbitals, (1, 0, 2))
    both = call(cut_rotation, (2, FAR, 32, WIDE), 0, 3 * FIELD, (V,))(rotation)
    both = lax.all_to_all(both, "y_hi", split_axis=0, concat_axis=0, tiled=True)
    cut = call(cut_columns, ((2 * ELEMS * PIECE, WIDE),) * LOW, 0, 2 * FIELD, (V,))(pieces)
    rows = [cut[0]] + [
        lax.ppermute(cut[by], "z_lo", [(i, (i + by) % LOW) for i in range(LOW)]) for by in range(1, LOW)
    ]
    message = (2 * PASS + 32, WIDE)
    up, down, slices = call(pack, (message, message, (64, WIDE)), 0, 6 * FIELD, (V,) * 5)(*rows, both)
    above, below = far_step(down, -1), far_step(up, 1)
    shapes = (hamiltonian.shape, hamiltonian.shape, (ROWS, WIDE))
    blocks = call(split_blocks, shapes, 0, 2 * BLOCKS, (V, S), (), BF16)(hamiltonian, counts)
    below, *blocks, live = lax.optimization_barrier((below, *blocks))
    passed_up, passed_down = far_step(below[:PASS], 1), far_step(above[:PASS], -1)
    mine = call(collect, (256, WIDE), 0, 4 * FIELD, (V,) * 5)(slices, below, above, passed_up, passed_down)
    other = lax.ppermute(mine, "core", [(0, 1), (1, 0)])
    scratch = [V((2, HALF, WIDE), F32)]
    parts = call(rotate, (NEAR, HALF, WIDE), 6 * 320 * 256 * 256, 11 * FIELD, (V,) * 8, scratch)(
        up, down, mine, other, below, above, passed_up, passed_down
    )
    parts = lax.all_to_all(parts, NEARS, split_axis=0, concat_axis=0, tiled=True)
    scratch = [V((2, HALF, WIDE), F32), V((40, WIDE), F32)]
    start = call(add_up, (ROWS, WIDE), 0, 5 * FIELD, (V, V), scratch)(parts, live)

    own = call(own_and_ring, (ROWS, WIDE), 6 * 20 * ROWS * ROWS * WIDE, BLOCKS, (V,) * 5)
    first = call(first_step, (ROWS, WIDE), 6 * 8 * ROWS * ROWS * WIDE, BLOCKS // 3, (V,) * 7 + (S,) * 2)
    second = call(second_step, (WIDE, ROWS), 6 * 8 * ROWS * ROWS * WIDE, BLOCKS // 3, (V,) * 8 + (S,) * 2)
    a, b, c, d = neighbours(start)
    own_part = own(start, a, b, *blocks)
    middle = first(own_part, c, d, *blocks, start, live, center, width)
    a, b, c, d = neighbours(middle)
    own_part = own(middle, a, b, *blocks)
    filtered = second(own_part, c, d, *blocks, middle, start, live, center, width)
    return jnp.transpose(filtered.reshape(ELEMS, BANDS, ROWS), (0, 2, 1))


def solution(mesh):
    inner = Mesh(
        mesh.devices.reshape(LAYERS, COLUMNS, CORES, FAR, NEAR // 2, 2), ELEM + BAND
    )
    return jax.shard_map(
        shards,
        mesh=inner,
        in_specs=(P(ELEM, BAND, None), P(BAND, None), P(ELEM), P(ELEM, None, None, None), P(), P()),
        out_specs=P(ELEM, None, BAND),
        check_vma=False,
    )
```

```python
import jax
import jax.numpy as jnp
from jax import lax
from jax.experimental import pallas as pl
from jax.experimental.pallas import tpu as pltpu
from jax.sharding import Mesh
from jax.sharding import PartitionSpec as P

LAYERS, COLUMNS, CORES = 4, 4, 2
FAR, NEAR = 4, 8
ELEMS, ROWS, WIDE = 4, 160, 128
BANDS = 32
PIECE = 5
ELEM = ("layer", "column", "core")
RING = ("column", "core")
NEARS = ("z_lo", "y_hi")
BAND = ("z_hi",) + NEARS
F32, BF16 = jnp.float32, jnp.bfloat16


def call(kernel, out, flops, moved, spaces, scratch=(), kind=F32):
    several = isinstance(out[0], tuple)
    shapes = tuple(jax.ShapeDtypeStruct(o, kind) for o in (out if several else (out,)))
    specs = tuple(pl.BlockSpec(memory_space=pltpu.VMEM) for _ in shapes)
    return pl.pallas_call(
        kernel,
        out_shape=shapes if several else shapes[0],
        in_specs=[pl.BlockSpec(memory_space=s) for s in spaces],
        out_specs=specs if several else specs[0],
        scratch_shapes=scratch,
        compiler_params=pltpu.CompilerParams(vmem_limit_bytes=32 << 20),
        cost_estimate=pl.CostEstimate(flops=flops, bytes_accessed=moved, transcendentals=0),
    )


def split(v):
    high = v.astype(BF16)
    return high, (v - high.astype(F32)).astype(BF16)


def dot3(a, b):
    def dot(x, y):
        return jnp.dot(x, y, preferred_element_type=F32)

    return dot(a[0], b[0]) + (dot(a[0], b[1]) + dot(a[1], b[0]))


def lane_owner(shape):
    return lax.broadcasted_iota(jnp.int32, shape, len(shape) - 1) // BANDS


def by_owner(parts):
    owner = lane_owner(parts[0].shape)
    picked = parts[0]
    for e in range(1, ELEMS):
        picked = jnp.where(owner == e, parts[e], picked)
    return picked


def turned(v, by):
    by = by % ELEMS
    return pltpu.roll(v, by * BANDS, 1) if by else v


def alive(counts_ref):
    owner = lane_owner((ROWS, WIDE))
    row = lax.broadcasted_iota(jnp.int32, (ROWS, WIDE), 0)
    limit = jnp.full((ROWS, WIDE), counts_ref[0], jnp.int32)
    for e in range(1, ELEMS):
        limit = jnp.where(owner == e, counts_ref[e], limit)
    return row < limit


def cut_columns(orbitals_ref, rotation_ref, out_ref, slices_ref):
    for far in range(FAR):
        for half in range(2):
            slices_ref[far, pl.ds(32 * half, 32), :] = rotation_ref[:, pl.ds(256 * far + 128 * half, 128)]
    for i in range(PIECE):
        for near in range(NEAR):
            half, place = divmod(near, ELEMS)
            parts = [
                turned(orbitals_ref[i, :, pl.ds(256 * far + 128 * half, 128)], far - place)
                for far in range(FAR)
            ]
            out_ref[near, pl.ds(ELEMS * i, ELEMS), :] = by_owner(parts)


def far_place(by):
    return lax.rem(lax.axis_index("z_hi") + by, FAR)


HALF = ROWS // 2
PASS = HALF + 32


def pack(rows_ref, slices_ref, up_ref, down_ref):
    for e in range(ELEMS):
        top, mine = divmod(e, 2)
        first, second = (down_ref, up_ref) if top else (up_ref, down_ref)
        for near in range(NEAR):
            for i in range(PIECE):
                at = 40 * mine + PIECE * near + i
                row = rows_ref[near, pl.ds(ELEMS * i + e, 1), :]
                first[pl.ds(at, 1), :] = row
                second[pl.ds(PASS + at, 1), :] = row
    opposite = far_place(2)
    up_ref[HALF:PASS, :] = slices_ref[opposite, :32, :]
    down_ref[HALF:PASS, :] = slices_ref[opposite, 32:, :]
    up_ref[PASS + HALF :, :] = slices_ref[far_place(1)]
    down_ref[PASS + HALF :, :] = slices_ref[far_place(3)]


def rotate(up_ref, down_ref, slices_ref, below_ref, above_ref, passed_up_ref, passed_down_ref, out_ref, left_ref, right_ref):
    own = slices_ref[far_place(0)]
    sides = [
        (0, own[:32], own[32:], up_ref[:HALF, :], down_ref[:HALF, :]),
        (3, below_ref[PASS + HALF : PASS + HALF + 32, :], below_ref[PASS + HALF + 32 :, :],
         below_ref[:HALF, :], below_ref[PASS : PASS + HALF, :]),
        (1, above_ref[PASS + HALF : PASS + HALF + 32, :], above_ref[PASS + HALF + 32 :, :],
         above_ref[PASS : PASS + HALF, :], above_ref[:HALF, :]),
        (2, passed_up_ref[HALF:, :], passed_down_ref[HALF:, :], passed_up_ref[:HALF, :], passed_down_ref[:HALF, :]),
    ]
    for by, left, right, _, _ in sides:
        at = pl.ds(pl.multiple_of(32 * far_place(by), 32), 32)
        left_ref[at, :] = left
        right_ref[at, :] = right
    halves = [split(left_ref[...]), split(right_ref[...])]
    for by, _, _, top, bottom in sides:
        rows = split(jnp.concatenate([top, bottom], axis=0))
        products = [dot3(rows, half) for half in halves]
        at = pl.ds(pl.multiple_of(40 * far_place(by), 8), 40)
        for near in range(NEAR):
            half, place = divmod(near, ELEMS)
            out_ref[near, at, :] = by_owner(
                [turned(products[half][40 * e : 40 * e + 40], e - place) for e in range(ELEMS)]
            )


def add_up(parts_ref, live_ref, out_ref):
    total = parts_ref[0]
    for near in range(1, NEAR):
        total = total + parts_ref[near]
    out_ref[...] = jnp.where(live_ref[...].astype(F32) > 0.5, total, 0.0)


def split_blocks(hamiltonian_ref, counts_ref, high_ref, low_ref, live_ref):
    live_ref[...] = jnp.where(alive(counts_ref), 1.0, 0.0).astype(BF16)
    for e in range(ELEMS):
        for slot in range(7):
            high_ref[e, slot], low_ref[e, slot] = split(hamiltonian_ref[e, slot])


def blocks_times(high_ref, low_ref, slots, fields):
    def dot(x, y):
        return jnp.dot(x, y, preferred_element_type=F32)

    fields = [split(f) for f in fields]
    pairs = [jnp.concatenate(f, axis=1) for f in fields]
    totals = []
    for e in range(ELEMS):
        wide = narrow = None
        for slot, field, pair in zip(slots, fields, pairs):
            first, second = dot(high_ref[e, slot], pair), dot(low_ref[e, slot], field[0])
            wide = first if wide is None else wide + first
            narrow = second if narrow is None else narrow + second
        totals.append(wide[:, :WIDE] + (wide[:, WIDE:] + narrow))
    return by_owner(totals)


def own_and_ring(field_ref, a_ref, b_ref, high_ref, low_ref, out_ref):
    field = field_ref[...]
    out_ref[...] = blocks_times(
        high_ref, low_ref, range(5), (field, turned(field, 1), turned(field, -1), a_ref[...], b_ref[...])
    )


def applied(own_ref, c_ref, d_ref, high_ref, low_ref, live_ref):
    total = own_ref[...] + blocks_times(high_ref, low_ref, (5, 6), (c_ref[...], d_ref[...]))
    return jnp.where(live_ref[...].astype(F32) > 0.5, total, 0.0)


def first_step(own_ref, c_ref, d_ref, high_ref, low_ref, start_ref, live_ref, center_ref, width_ref, out_ref):
    total = applied(own_ref, c_ref, d_ref, high_ref, low_ref, live_ref)
    out_ref[...] = (total - center_ref[0] * start_ref[...]) / width_ref[0]


def second_step(own_ref, c_ref, d_ref, high_ref, low_ref, middle_ref, start_ref, live_ref, center_ref, width_ref, out_ref):
    total = applied(own_ref, c_ref, d_ref, high_ref, low_ref, live_ref)
    filtered = 2.0 * (total - center_ref[0] * middle_ref[...]) / width_ref[0] - start_ref[...]
    out_ref[...] = jnp.transpose(filtered)


def neighbours(field):
    ring = COLUMNS * CORES
    return (
        lax.ppermute(field, RING, [(i, (i + 1) % ring) for i in range(ring)]),
        lax.ppermute(field, RING, [(i, (i - 1) % ring) for i in range(ring)]),
        lax.ppermute(field, "layer", [(i, i + 1) for i in range(LAYERS - 1)]),
        lax.ppermute(field, "layer", [(i + 1, i) for i in range(LAYERS - 1)]),
    )


def far_step(v, by):
    return lax.ppermute(v, "z_hi", [(i, (i + by) % FAR) for i in range(FAR)])


V, S = pltpu.VMEM, pltpu.SMEM
FIELD = ROWS * WIDE * 4
BLOCKS = ELEMS * 7 * ROWS * 256 * 4


def shards(orbitals, rotation, counts, hamiltonian, center, width):
    pieces = jnp.transpose(orbitals, (1, 0, 2))
    shapes = ((NEAR, ELEMS * PIECE, WIDE), (FAR, 64, WIDE))
    cut, slices = call(cut_columns, shapes, 0, 5 * FIELD, (V, V))(pieces, rotation)
    cut = lax.all_to_all(cut, NEARS, split_axis=0, concat_axis=0, tiled=True)
    message = (2 * PASS + 32, WIDE)
    up, down = call(pack, (message, message), 0, 6 * FIELD, (V, V))(cut, slices)
    above, below = far_step(down, -1), far_step(up, 1)
    shapes = (hamiltonian.shape, hamiltonian.shape, (ROWS, WIDE))
    blocks = call(split_blocks, shapes, 0, 2 * BLOCKS, (V, S), (), BF16)(hamiltonian, counts)
    below, *blocks, live = lax.optimization_barrier((below, *blocks))
    passed_up, passed_down = far_step(below[:PASS], 1), far_step(above[:PASS], -1)
    scratch = [V((WIDE, WIDE), F32)] * 2
    parts = call(rotate, (NEAR, ROWS, WIDE), 6 * 640 * 128 * 256, 13 * FIELD, (V,) * 7, scratch)(
        up, down, slices, below, above, passed_up, passed_down
    )
    parts = lax.all_to_all(parts, NEARS, split_axis=0, concat_axis=0, tiled=True)
    start = call(add_up, (ROWS, WIDE), 0, 9 * FIELD, (V, V))(parts, live)

    own = call(own_and_ring, (ROWS, WIDE), 6 * 20 * ROWS * ROWS * WIDE, BLOCKS, (V,) * 5)
    first = call(first_step, (ROWS, WIDE), 6 * 8 * ROWS * ROWS * WIDE, BLOCKS // 3, (V,) * 7 + (S,) * 2)
    second = call(second_step, (WIDE, ROWS), 6 * 8 * ROWS * ROWS * WIDE, BLOCKS // 3, (V,) * 8 + (S,) * 2)
    a, b, c, d = neighbours(start)
    own_part = own(start, a, b, *blocks)
    middle = first(own_part, c, d, *blocks, start, live, center, width)
    a, b, c, d = neighbours(middle)
    own_part = own(middle, a, b, *blocks)
    filtered = second(own_part, c, d, *blocks, middle, start, live, center, width)
    return jnp.transpose(filtered.reshape(ELEMS, BANDS, ROWS), (0, 2, 1))


def solution(mesh):
    inner = Mesh(
        mesh.devices.reshape(LAYERS, COLUMNS, CORES, FAR, NEAR // 2, 2), ELEM + BAND
    )
    return jax.shard_map(
        shards,
        mesh=inner,
        in_specs=(P(ELEM, BAND, None), P(BAND, None), P(ELEM), P(ELEM, None, None, None), P(), P()),
        out_specs=P(ELEM, None, BAND),
        check_vma=False,
    )
```

```python
import jax
import jax.numpy as jnp
from jax import lax
from jax.experimental import pallas as pl
from jax.experimental.pallas import tpu as pltpu
from jax.sharding import Mesh
from jax.sharding import PartitionSpec as P

LAYERS, COLUMNS, CORES = 4, 4, 2
FAR, LOW, NEAR = 4, 4, 8
ELEMS, ROWS, WIDE = 4, 160, 128
BANDS = 32
PIECE = 5
ELEM = ("layer", "column", "core")
RING = ("column", "core")
NEARS = ("z_lo", "y_hi")
BAND = ("z_hi",) + NEARS
F32, BF16 = jnp.float32, jnp.bfloat16


def call(kernel, out, flops, moved, spaces, scratch=(), kind=F32):
    several = isinstance(out[0], tuple)
    shapes = tuple(jax.ShapeDtypeStruct(o, kind) for o in (out if several else (out,)))
    specs = tuple(pl.BlockSpec(memory_space=pltpu.VMEM) for _ in shapes)
    return pl.pallas_call(
        kernel,
        out_shape=shapes if several else shapes[0],
        in_specs=[pl.BlockSpec(memory_space=s) for s in spaces],
        out_specs=specs if several else specs[0],
        scratch_shapes=scratch,
        compiler_params=pltpu.CompilerParams(vmem_limit_bytes=32 << 20),
        cost_estimate=pl.CostEstimate(flops=flops, bytes_accessed=moved, transcendentals=0),
    )


def split(v):
    high = v.astype(BF16)
    return high, (v - high.astype(F32)).astype(BF16)


def dot3(a, b):
    def dot(x, y):
        return jnp.dot(x, y, preferred_element_type=F32)

    return dot(a[0], b[0]) + (dot(a[0], b[1]) + dot(a[1], b[0]))


def lane_owner(shape):
    return lax.broadcasted_iota(jnp.int32, shape, len(shape) - 1) // BANDS


def by_owner(parts):
    owner = lane_owner(parts[0].shape)
    picked = parts[0]
    for e in range(1, ELEMS):
        picked = jnp.where(owner == e, parts[e], picked)
    return picked


def turned(v, by):
    by = by % ELEMS
    return pltpu.roll(v, by * BANDS, 1) if by else v


def alive(counts_ref):
    owner = lane_owner((ROWS, WIDE))
    row = lax.broadcasted_iota(jnp.int32, (ROWS, WIDE), 0)
    limit = jnp.full((ROWS, WIDE), counts_ref[0], jnp.int32)
    for e in range(1, ELEMS):
        limit = jnp.where(owner == e, counts_ref[e], limit)
    return row < limit


def cut_rotation(rotation_ref, mine_ref):
    for far in range(FAR):
        lanes = pl.ds(pl.multiple_of(256 * far + 128 * lax.axis_index("core"), 128), 128)
        mine_ref[far] = rotation_ref[:, lanes]


def cut_columns(orbitals_ref, out_ref):
    first = lax.broadcasted_iota(jnp.int32, (ELEMS, WIDE), 1) < 64
    for i in range(PIECE):
        for low in range(LOW):
            half, odd = divmod(low, 2)
            for k in range(2):
                parts = [orbitals_ref[i, :, pl.ds(256 * far + 128 * half, 128)] for far in (2 * k, 2 * k + 1)]
                parts[1 - odd] = turned(parts[1 - odd], 2)
                out_ref[low, pl.ds(20 * k + ELEMS * i, ELEMS), :] = jnp.where(first, parts[0], parts[1])


def far_place(by):
    return lax.rem(lax.axis_index("z_hi") + by, FAR)


HALF = ROWS // 2
PASS = HALF + 32


def pack(rows_ref, mine_ref, other_ref, up_ref, down_ref, own_ref):
    for k in range(2):
        first, second = (down_ref, up_ref) if k else (up_ref, down_ref)
        for e in range(ELEMS):
            for low in range(LOW):
                for i in range(PIECE):
                    at = 20 * e + PIECE * low + i
                    row = rows_ref[low, pl.ds(20 * k + ELEMS * i + e, 1), :]
                    first[pl.ds(at, 1), :] = row
                    second[pl.ds(PASS + at, 1), :] = row
    lower = lax.axis_index("y_hi") == 0

    def slices(by):
        mine, other = mine_ref[far_place(by)], other_ref[far_place(by)]
        return jnp.where(lower, mine, other), jnp.where(lower, other, mine)

    up_ref[HALF:PASS, :], down_ref[HALF:PASS, :] = slices(2)
    tail = PASS + HALF
    up_ref[tail : tail + 32, :], up_ref[tail + 32 :, :] = slices(1)
    down_ref[tail : tail + 32, :], down_ref[tail + 32 :, :] = slices(3)
    own_ref[:32, :], own_ref[32:, :] = slices(0)


def collect(own_ref, below_ref, above_ref, passed_up_ref, passed_down_ref, out_ref):
    tail = PASS + HALF
    passed = jnp.concatenate([passed_up_ref[HALF:, :], passed_down_ref[HALF:, :]], axis=0)
    for by, piece in ((0, own_ref[...]), (3, below_ref[tail:, :]), (1, above_ref[tail:, :]), (2, passed)):
        out_ref[pl.ds(pl.multiple_of(64 * far_place(by), 64), 64), :] = piece


def rotate(
    up_ref, down_ref, mine_ref, other_ref, below_ref, above_ref, passed_up_ref, passed_down_ref, out_ref, sum_ref
):
    tail = PASS + HALF
    sides = [
        (0, up_ref[:HALF, :], down_ref[:HALF, :]),
        (3, below_ref[:HALF, :], below_ref[PASS:tail, :]),
        (1, above_ref[PASS:tail, :], above_ref[:HALF, :]),
        (2, passed_up_ref[:HALF, :], passed_down_ref[:HALF, :]),
    ]
    first = lax.axis_index("core") == 0
    mine, other = mine_ref[...], other_ref[...]
    halves = [split(jnp.where(first, mine, other)), split(jnp.where(first, other, mine))]
    for by, top, bottom in sides:
        rows = split(jnp.concatenate([top, bottom], axis=1))
        for half in range(2):
            sum_ref[half] = dot3(rows, halves[half])
        for near in range(NEAR):
            half, place = divmod(near, ELEMS)
            out_ref[near, pl.ds(20 * by, 20), :] = by_owner(
                [turned(sum_ref[half, pl.ds(20 * e, 20), :], e - place) for e in range(ELEMS)]
            )


def add_up(parts_ref, live_ref, out_ref, sum_ref, rows_ref):
    for share in range(2):
        total = parts_ref[share]
        for low in range(1, LOW):
            total = total + parts_ref[2 * low + share]
        sum_ref[share] = total
    for by in range(FAR):
        for share in range(2):
            for low in range(LOW):
                rows_ref[pl.ds(10 * low + PIECE * share, PIECE), :] = sum_ref[share, pl.ds(20 * by + PIECE * low, PIECE), :]
        at = pl.ds(pl.multiple_of(40 * far_place(by), 8), 40)
        out_ref[at, :] = jnp.where(live_ref[at, :].astype(F32) > 0.5, rows_ref[...], 0.0)


def split_blocks(hamiltonian_ref, counts_ref, high_ref, low_ref, live_ref):
    live_ref[...] = jnp.where(alive(counts_ref), 1.0, 0.0).astype(BF16)
    for e in range(ELEMS):
        for slot in range(7):
            high_ref[e, slot], low_ref[e, slot] = split(hamiltonian_ref[e, slot])


def blocks_times(high_ref, low_ref, slots, fields):
    def dot(x, y):
        return jnp.dot(x, y, preferred_element_type=F32)

    fields = [split(f) for f in fields]
    pairs = [jnp.concatenate(f, axis=1) for f in fields]
    totals = []
    for e in range(ELEMS):
        wide = narrow = None
        for slot, field, pair in zip(slots, fields, pairs):
            first, second = dot(high_ref[e, slot], pair), dot(low_ref[e, slot], field[0])
            wide = first if wide is None else wide + first
            narrow = second if narrow is None else narrow + second
        totals.append(wide[:, :WIDE] + (wide[:, WIDE:] + narrow))
    return by_owner(totals)


def own_and_ring(field_ref, a_ref, b_ref, high_ref, low_ref, out_ref):
    field = field_ref[...]
    out_ref[...] = blocks_times(
        high_ref, low_ref, range(5), (field, turned(field, 1), turned(field, -1), a_ref[...], b_ref[...])
    )


def applied(own_ref, c_ref, d_ref, high_ref, low_ref, live_ref):
    odd = lax.rem(lax.axis_index("layer"), 2)
    total = own_ref[...] + blocks_times(high_ref, low_ref, (6 - odd, 5 + odd), (c_ref[...], d_ref[...]))
    return jnp.where(live_ref[...].astype(F32) > 0.5, total, 0.0)


def first_step(own_ref, c_ref, d_ref, high_ref, low_ref, start_ref, live_ref, center_ref, width_ref, out_ref):
    total = applied(own_ref, c_ref, d_ref, high_ref, low_ref, live_ref)
    out_ref[...] = (total - center_ref[0] * start_ref[...]) / width_ref[0]


def second_step(own_ref, c_ref, d_ref, high_ref, low_ref, middle_ref, start_ref, live_ref, center_ref, width_ref, out_ref):
    total = applied(own_ref, c_ref, d_ref, high_ref, low_ref, live_ref)
    filtered = 2.0 * (total - center_ref[0] * middle_ref[...]) / width_ref[0] - start_ref[...]
    out_ref[...] = jnp.transpose(filtered)


def neighbours(field):
    ring = COLUMNS * CORES
    return (
        lax.ppermute(field, RING, [(i, (i + 1) % ring) for i in range(ring)]),
        lax.ppermute(field, RING, [(i, (i - 1) % ring) for i in range(ring)]),
        lax.ppermute(field, "layer", [(i, i ^ 1) for i in range(LAYERS)]),
        lax.ppermute(field, "layer", [(i, LAYERS - 1 - i) for i in range(1, LAYERS - 1)]),
    )


def far_step(v, by):
    return lax.ppermute(v, "z_hi", [(i, (i + by) % FAR) for i in range(FAR)])


V, S = pltpu.VMEM, pltpu.SMEM
FIELD = ROWS * WIDE * 4
BLOCKS = ELEMS * 7 * ROWS * 256 * 4


def shards(orbitals, rotation, counts, hamiltonian, center, width):
    pieces = jnp.transpose(orbitals, (1, 0, 2))
    mine = call(cut_rotation, (FAR, 32, WIDE), 0, 2 * FIELD, (V,))(rotation)
    other = lax.ppermute(mine, "y_hi", [(0, 1), (1, 0)])
    cut = call(cut_columns, (LOW, 2 * ELEMS * PIECE, WIDE), 0, 2 * FIELD, (V,))(pieces)
    cut = lax.all_to_all(cut, "z_lo", split_axis=0, concat_axis=0, tiled=True)
    message = (2 * PASS + 32, WIDE)
    up, down, slices = call(pack, (message, message, (64, WIDE)), 0, 6 * FIELD, (V,) * 3)(cut, mine, other)
    above, below = far_step(down, -1), far_step(up, 1)
    shapes = (hamiltonian.shape, hamiltonian.shape, (ROWS, WIDE))
    blocks = call(split_blocks, shapes, 0, 2 * BLOCKS, (V, S), (), BF16)(hamiltonian, counts)
    below, *blocks, live = lax.optimization_barrier((below, *blocks))
    passed_up, passed_down = far_step(below[:PASS], 1), far_step(above[:PASS], -1)
    mine = call(collect, (256, WIDE), 0, 4 * FIELD, (V,) * 5)(slices, below, above, passed_up, passed_down)
    other = lax.ppermute(mine, "core", [(0, 1), (1, 0)])
    scratch = [V((2, HALF, WIDE), F32)]
    parts = call(rotate, (NEAR, HALF, WIDE), 6 * 320 * 256 * 256, 11 * FIELD, (V,) * 8, scratch)(
        up, down, mine, other, below, above, passed_up, passed_down
    )
    parts = lax.all_to_all(parts, NEARS, split_axis=0, concat_axis=0, tiled=True)
    scratch = [V((2, HALF, WIDE), F32), V((40, WIDE), F32)]
    start = call(add_up, (ROWS, WIDE), 0, 5 * FIELD, (V, V), scratch)(parts, live)

    own = call(own_and_ring, (ROWS, WIDE), 6 * 20 * ROWS * ROWS * WIDE, BLOCKS, (V,) * 5)
    first = call(first_step, (ROWS, WIDE), 6 * 8 * ROWS * ROWS * WIDE, BLOCKS // 3, (V,) * 7 + (S,) * 2)
    second = call(second_step, (WIDE, ROWS), 6 * 8 * ROWS * ROWS * WIDE, BLOCKS // 3, (V,) * 8 + (S,) * 2)
    a, b, c, d = neighbours(start)
    own_part = own(start, a, b, *blocks)
    middle = first(own_part, c, d, *blocks, start, live, center, width)
    a, b, c, d = neighbours(middle)
    own_part = own(middle, a, b, *blocks)
    filtered = second(own_part, c, d, *blocks, middle, start, live, center, width)
    return jnp.transpose(filtered.reshape(ELEMS, BANDS, ROWS), (0, 2, 1))


def solution(mesh):
    inner = Mesh(
        mesh.devices.reshape(LAYERS, COLUMNS, CORES, FAR, NEAR // 2, 2), ELEM + BAND
    )
    return jax.shard_map(
        shards,
        mesh=inner,
        in_specs=(P(ELEM, BAND, None), P(BAND, None), P(ELEM), P(ELEM, None, None, None), P(), P()),
        out_specs=P(ELEM, None, BAND),
        check_vma=False,
    )
```
